512 devices in a mesh: band: 128 (over z, y, x_lo), domain: 4 (over x_hi, core).
Axes of the slice: x: 4 (x_hi: 2, x_lo: 2; x = x_hi * 2 + x_lo), y: 4, z: 16, core: 2. Of those that a mesh axis runs over, the one named last changes fastest.
Arguments:
- orbitals: bfloat16 [1024, 8, 5120], P('band', 'domain'), may hold values from -6 to 6
- boundary: bfloat16 [1024, 4, 5120], P('band'), may hold values from -6 to 6
- potential: bfloat16 [8, 5120], P('domain'), may hold values from 0 to 2
Outputs:
- correlation: float32 [1024, 1024], P('band', 'domain')
- projected: float32 [1024, 1024], P('band', 'domain')
The draws below stay inside these ranges and needn't reach their ends.
All inputs are finite; a program needn't handle non-finite values.
Results may differ from the reference program's by a relative error of at most 0.0012.
Values may be sent and summed in bfloat16 or wider, within the bound.
No kernel may reach another device: no remote copies, remote signals or barrier semaphores. Data moves between devices by JAX's collectives and lax.ppermute only.
A program may use at most 128 MiB of HBM per device.

```python
import math
import jax
import jax.numpy as jnp
from jax import lax

NORB = 1024
NX = 160
NY = 32
DEGREE = 4
NZ = 8
PLANE = 5120


def level_of(rng, dims, split, least, largest):
    def one(axis_at, parts):
        draws = jax.random.uniform(jax.random.fold_in(jax.random.fold_in(rng, 6), axis_at), (parts,), jnp.float32, least / len(split), largest / len(split))
        return jnp.repeat(jnp.exp(draws), dims[axis_at] // parts).reshape((-1,) + (1,) * (len(dims) - axis_at - 1))

    level = one(*split[0])
    for cut in split[1:]:
        level = level * one(*cut)
    return level


def noise(stream_key, dims, deviation, reach, cuts=(), dtype=jnp.bfloat16):
    array = jax.random.normal(stream_key, dims, jnp.float32) * deviation
    if len(cuts) > 0:
        array = level_of(stream_key, dims, cuts, -0.22, 0.18) * array
    return jnp.clip(array, min=-reach, max=reach).astype(dtype)


def setup_inputs(seed: int = 0) -> dict:
    keys = jax.random.split(jax.random.key(seed), 4)
    return {
        "orbitals": noise(keys[0], (NORB, NZ, PLANE), 1.0, 6.0, ((0, 128), (1, 4))),
        "boundary": noise(keys[1], (NORB, 4, PLANE), 1.0, 6.0, ((0, 128),)),
        "potential": jnp.clip(2.0 * jax.random.uniform(keys[2], (NZ, PLANE), jnp.float32) ** level_of(keys[2], (NZ, PLANE), ((0, 4),), -0.2, 0.2), 0.0, 2.0).astype(jnp.bfloat16),
    }


filter_center = 5.5
filter_radius = 4.5


def second_diff(values, axis_pos):
    near = jnp.roll(values, 1, axis_pos) + jnp.roll(values, -1, axis_pos)
    far = jnp.roll(values, 2, axis_pos) + jnp.roll(values, -2, axis_pos)
    return (16.0 * near - far - 30.0 * values) / 12.0


def plane_part(values):
    shaped = values.reshape(values.shape[:-1] + (NY, NX))
    total = second_diff(shaped, -1) + second_diff(shaped, -2)
    return total.reshape(values.shape)


def hamiltonian(padded, potential):
    middle = padded[:, 2:-2]
    z_part = (16.0 * (padded[:, 1:-3] + padded[:, 3:-1]) - (padded[:, :-4] + padded[:, 4:]) - 30.0 * middle) / 12.0
    laplace = z_part + plane_part(middle)
    return -0.5 * laplace + potential.astype(jnp.float32) * middle


def chebyshev(apply_ham, orb_block):
    earlier = orb_block
    current = ((apply_ham(orb_block) - filter_center * orb_block.astype(jnp.float32)) / filter_radius).astype(jnp.bfloat16)
    for degree_step in range(DEGREE - 1):
        following = 2.0 * (apply_ham(current) - filter_center * current.astype(jnp.float32)) / filter_radius
        following = (following - earlier.astype(jnp.float32)).astype(jnp.bfloat16)
        earlier, current = current, following
    return current, apply_ham(current).astype(jnp.bfloat16)


def reference(orbitals, boundary, potential):
    group_size = math.gcd(NORB, 64)

    def one_group(pieces):
        orb_block, rim_planes = pieces

        def apply_ham(values):
            padded = jnp.concatenate([rim_planes[:, 0:2], values, rim_planes[:, 2:4]], axis=1).astype(jnp.float32)
            return hamiltonian(padded, potential)

        return chebyshev(apply_ham, orb_block)

    grouped = (orbitals.reshape(NORB // group_size, group_size, NZ, NY * NX),
               boundary.reshape(NORB // group_size, group_size, 4, NY * NX))
    filtered, applied = lax.map(one_group, grouped)
    filtered = filtered.reshape(NORB, NZ * NY * NX).astype(jnp.float32)
    applied = applied.reshape(NORB, NZ * NY * NX).astype(jnp.float32)
    total_cells = NZ * NY * NX
    correlation = jnp.dot(filtered, filtered.T, precision=lax.Precision.HIGHEST) / total_cells
    projected = jnp.dot(filtered, applied.T, precision=lax.Precision.HIGHEST) / total_cells
    return correlation, projected
```

```python
import functools
import jax
import jax.numpy as jnp
from jax import lax
from jax.experimental import pallas as pl
from jax.experimental.pallas import tpu as pltpu
from jax.sharding import Mesh, PartitionSpec as P

NX = 160
NY = 32
NZ = 8
PLANE = NX * NY
DEGREE = 4
ORBS = 8
PAD = 384
SPAN = 640
CHUNKS = PLANE // SPAN
SHARES = 32
SHARE = NZ * PLANE // SHARES

filter_center = 5.5
filter_radius = 4.5


def filter_kernel(which, mixed_ref, rim_ref, out_ref, one, two, rim_term, pot):
    del which
    row = lax.broadcasted_iota(jnp.int32, (NZ, SPAN), 0)
    x = lax.rem(lax.broadcasted_iota(jnp.int32, (NZ, SPAN), 1), NX)
    zero = jnp.zeros((NZ, SPAN), jnp.float32)
    below_1 = jnp.where(row >= 1, zero + 16.0, zero)
    above_1 = jnp.where(row <= NZ - 2, zero + 16.0, zero)
    below_2 = jnp.where(row >= 2, zero + 1.0, zero)
    above_2 = jnp.where(row <= NZ - 3, zero + 1.0, zero)
    first, last = x == 0, x == NX - 1
    first_two, last_two = x <= 1, x >= NX - 2

    def wrap(ref, orb):
        ref[orb, :, 0:PAD] = ref[orb, :, PLANE : PLANE + PAD]
        ref[orb, :, PAD + PLANE : 2 * PAD + PLANE] = ref[orb, :, PAD : 2 * PAD]

    pot[...] = jnp.concatenate([mixed_ref[s, 4:6, :] for s in range(4)], axis=0).astype(jnp.float32)
    for orb in range(2):
        planes = [mixed_ref[s, 2 * orb : 2 * orb + 2, :] for s in range(4)]
        one[orb, :, PAD : PAD + PLANE] = jnp.concatenate(planes, axis=0).astype(jnp.float32)
        wrap(one, orb)
        rim = rim_ref[0, orb].astype(jnp.float32)
        low_far, low, high, high_far = (rim[k : k + 1] for k in range(4))
        rim_term[orb] = jnp.concatenate(
            [16.0 * low - low_far, -low, jnp.zeros((4, PLANE), jnp.float32), -high, 16.0 * high - high_far],
            axis=0,
        )

    def apply_ham(ref, orb, at):
        window = ref[orb, :, pl.ds(at, SPAN + 2 * PAD)]
        width = SPAN + 2 * PAD

        def cells(shift):
            return pltpu.roll(window, (-shift) % width, 1)[:, PAD : PAD + SPAN]

        middle = window[:, PAD : PAD + SPAN]
        near = jnp.where(first, cells(NX - 1), cells(-1)) + jnp.where(last, cells(1 - NX), cells(1))
        near = near + (cells(NX) + cells(-NX))
        far = jnp.where(first_two, cells(NX - 2), cells(-2)) + jnp.where(
            last_two, cells(2 - NX), cells(2)
        )
        far = far + (cells(2 * NX) + cells(-2 * NX))
        z_near = below_1 * pltpu.roll(middle, 1, 0) + above_1 * pltpu.roll(middle, NZ - 1, 0)
        z_far = below_2 * pltpu.roll(middle, 2, 0) + above_2 * pltpu.roll(middle, NZ - 2, 0)
        total = (16.0 * near - far) + (z_near - z_far) - 90.0 * middle
        total = total + rim_term[orb, :, pl.ds(at, SPAN)]
        return total * (-0.5 / 12.0) + pot[:, pl.ds(at, SPAN)] * middle, middle

    current, earlier = one, two
    for step in range(DEGREE):

        def body(chunk, carry, step=step, current=current, earlier=earlier):
            at = pl.multiple_of(chunk * SPAN, SPAN)
            for orb in range(2):
                with_h, middle = apply_ham(current, orb, at)
                following = (with_h - filter_center * middle) * (1.0 / filter_radius)
                place = (orb, slice(None), pl.ds(at + PAD, SPAN))
                if step > 0:
                    following = 2.0 * following - earlier[place]
                earlier[place] = following.astype(jnp.bfloat16).astype(jnp.float32)
            return carry

        lax.fori_loop(0, CHUNKS, body, 0)
        for orb in range(2):
            wrap(earlier, orb)
        current, earlier = earlier, current

    def last_body(chunk, carry):
        at = pl.multiple_of(chunk * SPAN, SPAN)
        for orb in range(2):
            with_h, middle = apply_ham(current, orb, at)
            out_ref[orb, :, pl.ds(at, SPAN)] = middle.astype(jnp.bfloat16)
            out_ref[2 + orb, :, pl.ds(at, SPAN)] = with_h.astype(jnp.bfloat16)
        return carry

    lax.fori_loop(0, CHUNKS, last_body, 0)


def filtered_and_applied(which, mixed, boundary):
    return pl.pallas_call(
        filter_kernel,
        grid_spec=pltpu.PrefetchScalarGridSpec(
            num_scalar_prefetch=1,
            grid=(1,),
            in_specs=[
                pl.BlockSpec((4, 6, PLANE), lambda i, which: (0, 0, 0)),
                pl.BlockSpec((1, 2, 4, PLANE), lambda i, which: (which[0], 0, 0, 0)),
            ],
            out_specs=pl.BlockSpec((4, NZ, PLANE), lambda i, which: (0, 0, 0)),
            scratch_shapes=[
                pltpu.VMEM((2, NZ, PLANE + 2 * PAD), jnp.float32),
                pltpu.VMEM((2, NZ, PLANE + 2 * PAD), jnp.float32),
                pltpu.VMEM((2, NZ, PLANE), jnp.float32),
                pltpu.VMEM((NZ, PLANE), jnp.float32),
            ],
        ),
        out_shape=jax.ShapeDtypeStruct((4, NZ, PLANE), jnp.bfloat16),
        compiler_params=pltpu.CompilerParams(vmem_limit_bytes=24 * 1024 * 1024),
        name="chebyshev_filter",
    )(which, mixed, boundary)


def per_device(orbitals, boundary, potential, trade):
    own = lax.axis_index("d")
    pieces = orbitals.reshape(4, 4, PLANE)
    pieces = jnp.concatenate([pieces, jnp.broadcast_to(potential[None], (4, 2, PLANE))], axis=1)
    mixed = lax.all_to_all(pieces, "d", split_axis=0, concat_axis=0, tiled=True)
    fields = filtered_and_applied(
        own.astype(jnp.int32).reshape(1), mixed, boundary.reshape(4, 2, 4, PLANE)
    )
    shares = fields.reshape(4, SHARES, SHARE).transpose(1, 0, 2)
    shares = lax.all_to_all(shares, ("y", "xl", "d"), split_axis=0, concat_axis=0, tiled=True)
    shares = shares.reshape(SHARES, 2, 2, SHARE).transpose(1, 0, 2, 3).reshape(2, 64, SHARE)
    columns = lax.all_gather(shares, "zl", axis=1, tiled=True).reshape(512, SHARE)
    rows = lax.all_gather(shares[0], "zh", axis=0, tiled=True)
    partial = lax.dot_general(
        rows, columns, (((1,), (1,)), ((), ())), preferred_element_type=jnp.float32
    )
    partial = partial.reshape(4, 8, ORBS, 512).transpose(1, 0, 2, 3).reshape(SHARES, ORBS, 512)
    parts = lax.all_to_all(partial, ("y", "xl", "d"), split_axis=0, concat_axis=0, tiled=True)
    summed = jnp.sum(parts, axis=0) * (1.0 / (NZ * PLANE))
    summed = lax.ppermute(summed, ("zh", "zl", "y", "xl", "d"), trade)
    return summed[:, :256], summed[:, 256:]


def solution(mesh):
    split = Mesh(mesh.devices.reshape(4, 4, 4, 2, 4), ("zh", "zl", "y", "xl", "d"))
    trade = []
    for zh in range(4):
        for rest in range(32):
            for d in range(4):
                trade.append(((zh * 32 + rest) * 4 + d, (d * 32 + rest) * 4 + zh))
    band = ("zh", "zl", "y", "xl")
    return jax.shard_map(
        functools.partial(per_device, trade=trade),
        mesh=split,
        in_specs=(P(band, "d", None), P(band, None, None), P("d", None)),
        out_specs=(P(band, "d"), P(band, "d")),
        check_vma=False,
    )
```

```python
import jax
import jax.numpy as jnp
from jax import lax
from jax.experimental import pallas as pl
from jax.experimental.pallas import tpu as pltpu
from jax.sharding import Mesh, PartitionSpec as P

NX = 160
NY = 32
NZ = 8
PLANE = NX * NY
DEGREE = 4
PAD = 384
SPAN = 640
CHUNKS = PLANE // SPAN
SHARES = 16
SHARE = NZ * PLANE // SHARES

filter_center = 5.5
filter_radius = 4.5


def filter_kernel(which, mixed_ref, rim_ref, out_ref, one, two, rim_term, pot):
    del which
    row = lax.broadcasted_iota(jnp.int32, (NZ, SPAN), 0)
    x = lax.rem(lax.broadcasted_iota(jnp.int32, (NZ, SPAN), 1), NX)
    zero = jnp.zeros((NZ, SPAN), jnp.float32)
    below_1 = jnp.where(row >= 1, zero + 16.0, zero)
    above_1 = jnp.where(row <= NZ - 2, zero + 16.0, zero)
    below_2 = jnp.where(row >= 2, zero + 1.0, zero)
    above_2 = jnp.where(row <= NZ - 3, zero + 1.0, zero)
    first, last = x == 0, x == NX - 1
    first_two, last_two = x <= 1, x >= NX - 2

    def wrap(ref, orb):
        ref[orb, :, 0:PAD] = ref[orb, :, PLANE : PLANE + PAD]
        ref[orb, :, PAD + PLANE : 2 * PAD + PLANE] = ref[orb, :, PAD : 2 * PAD]

    pot[...] = jnp.concatenate([mixed_ref[s, 4:6, :] for s in range(4)], axis=0).astype(jnp.float32)
    for orb in range(2):
        planes = [mixed_ref[s, 2 * orb : 2 * orb + 2, :] for s in range(4)]
        one[orb, :, PAD : PAD + PLANE] = jnp.concatenate(planes, axis=0).astype(jnp.float32)
        wrap(one, orb)
        rim = rim_ref[0, orb].astype(jnp.float32)
        low_far, low, high, high_far = (rim[k : k + 1] for k in range(4))
        rim_term[orb] = jnp.concatenate(
            [16.0 * low - low_far, -low, jnp.zeros((4, PLANE), jnp.float32), -high, 16.0 * high - high_far],
            axis=0,
        )

    def apply_ham(ref, orb, at):
        window = ref[orb, :, pl.ds(at, SPAN + 2 * PAD)]
        width = SPAN + 2 * PAD

        def cells(shift):
            return pltpu.roll(window, (-shift) % width, 1)[:, PAD : PAD + SPAN]

        middle = window[:, PAD : PAD + SPAN]
        near = jnp.where(first, cells(NX - 1), cells(-1)) + jnp.where(last, cells(1 - NX), cells(1))
        near = near + (cells(NX) + cells(-NX))
        far = jnp.where(first_two, cells(NX - 2), cells(-2)) + jnp.where(
            last_two, cells(2 - NX), cells(2)
        )
        far = far + (cells(2 * NX) + cells(-2 * NX))
        z_near = below_1 * pltpu.roll(middle, 1, 0) + above_1 * pltpu.roll(middle, NZ - 1, 0)
        z_far = below_2 * pltpu.roll(middle, 2, 0) + above_2 * pltpu.roll(middle, NZ - 2, 0)
        total = (16.0 * near - far) + (z_near - z_far) - 90.0 * middle
        total = total + rim_term[orb, :, pl.ds(at, SPAN)]
        return total * (-0.5 / 12.0) + pot[:, pl.ds(at, SPAN)] * middle, middle

    current, earlier = one, two
    for step in range(DEGREE):

        def body(chunk, carry, step=step, current=current, earlier=earlier):
            at = chunk * SPAN
            for orb in range(2):
                with_h, middle = apply_ham(current, orb, at)
                following = (with_h - filter_center * middle) * (1.0 / filter_radius)
                place = (orb, slice(None), pl.ds(at + PAD, SPAN))
                if step > 0:
                    following = 2.0 * following - earlier[place]
                earlier[place] = following.astype(jnp.bfloat16).astype(jnp.float32)
            return carry

        for chunk in range(CHUNKS):
            body(chunk, 0)
        for orb in range(2):
            wrap(earlier, orb)
        current, earlier = earlier, current

    def last_body(chunk, carry):
        at = chunk * SPAN
        for orb in range(2):
            with_h, middle = apply_ham(current, orb, at)
            out_ref[orb, :, pl.ds(at, SPAN)] = middle.astype(jnp.bfloat16)
            out_ref[2 + orb, :, pl.ds(at, SPAN)] = with_h.astype(jnp.bfloat16)
        return carry

    for chunk in range(CHUNKS):
        last_body(chunk, 0)


def filtered_and_applied(which, mixed, boundary):
    return pl.pallas_call(
        filter_kernel,
        grid_spec=pltpu.PrefetchScalarGridSpec(
            num_scalar_prefetch=1,
            grid=(1,),
            in_specs=[
                pl.BlockSpec((4, 6, PLANE), lambda i, which: (0, 0, 0)),
                pl.BlockSpec((1, 2, 4, PLANE), lambda i, which: (which[0], 0, 0, 0)),
            ],
            out_specs=pl.BlockSpec((4, NZ, PLANE), lambda i, which: (0, 0, 0)),
            scratch_shapes=[
                pltpu.VMEM((2, NZ, PLANE + 2 * PAD), jnp.float32),
                pltpu.VMEM((2, NZ, PLANE + 2 * PAD), jnp.float32),
                pltpu.VMEM((2, NZ, PLANE), jnp.float32),
                pltpu.VMEM((NZ, PLANE), jnp.float32),
            ],
        ),
        out_shape=jax.ShapeDtypeStruct((4, NZ, PLANE), jnp.bfloat16),
        compiler_params=pltpu.CompilerParams(vmem_limit_bytes=24 * 1024 * 1024),
        name="chebyshev_filter",
    )(which, mixed, boundary)


def picked(source, values):
    count = values.shape[0]
    hot = lax.broadcasted_iota(jnp.int32, (count, count), 1) == source
    hot = jnp.where(hot, 1.0, 0.0).astype(jnp.bfloat16)
    return jnp.dot(hot, values, preferred_element_type=jnp.float32).astype(jnp.bfloat16)


def product_kernel(core_ref, own_ref, other_ref, cols_ref, out_ref):
    core = core_ref[0]
    at = lax.broadcasted_iota(jnp.int32, (256, 256), 0)
    z, xl, xh, c, r = at // 16, at // 8 % 2, at // 4 % 2, at // 2 % 2, at % 2
    half = jnp.where(c == core, 0, 1)
    rows = picked(
        (((half * 2 + xl) * 2 + xh) * 16 + z) * 2 + r,
        jnp.concatenate([own_ref[...], other_ref[...]], axis=0),
    )
    zh, which, y, zl, r = at // 64, at // 32 % 2, at // 8 % 4, at // 2 % 4, at % 2
    cols = picked(((y * 16 + zh * 4 + zl) * 2 + which) * 2 + r, cols_ref[...])
    block = lax.dot_general(
        rows, cols, (((1,), (1,)), ((), ())), preferred_element_type=jnp.float32
    )
    for group in range(32):
        for zh in range(4):
            out_ref[group * 4 + zh] = block[8 * group : 8 * group + 8, 64 * zh : 64 * zh + 64]


def block_product(core, own, other, cols):
    whole = pl.BlockSpec(memory_space=pltpu.VMEM)
    return pl.pallas_call(
        product_kernel,
        in_specs=[pl.BlockSpec(memory_space=pltpu.SMEM), whole, whole, whole],
        out_specs=whole,
        out_shape=jax.ShapeDtypeStruct((128, 8, 64), jnp.float32),
        compiler_params=pltpu.CompilerParams(vmem_limit_bytes=32 * 1024 * 1024),
        name="block_product",
    )(core, own, other, cols)


def finish_kernel(parts_ref, correlation_ref, projected_ref):
    total = parts_ref[0]
    for k in range(1, 16):
        total = total + parts_ref[k]
    total = total * (1.0 / (NZ * PLANE))
    given = jnp.concatenate([total[k] for k in range(8)], axis=1)
    at = lax.broadcasted_iota(jnp.int32, (512, 512), 1)
    which, zl, y, xl, d, r = at // 256, at // 64 % 4, at // 16 % 4, at // 8 % 2, at // 2 % 4, at % 2
    source = (xl * 4 + d) * 64 + ((which * 4 + y) * 4 + zl) * 2 + r
    hot = jnp.where(lax.broadcasted_iota(jnp.int32, (512, 512), 0) == source, 1.0, 0.0)
    placed = jnp.dot(
        given, hot, preferred_element_type=jnp.float32, precision=lax.Precision.HIGHEST
    )
    correlation_ref[...] = placed[:, :256]
    projected_ref[...] = placed[:, 256:]


def finish(parts):
    shape = jax.ShapeDtypeStruct((8, 256), jnp.float32)
    whole = pl.BlockSpec(memory_space=pltpu.VMEM)
    return pl.pallas_call(
        finish_kernel,
        in_specs=[whole],
        out_specs=[whole, whole],
        out_shape=[shape, shape],
        name="finish",
    )(parts)


def per_device(orbitals, boundary, potential):
    own = lax.axis_index("xh") * 2 + lax.axis_index("c")
    pieces = orbitals.reshape(4, 4, PLANE)
    pieces = jnp.concatenate([pieces, jnp.broadcast_to(potential[None], (4, 2, PLANE))], axis=1)
    mixed = lax.all_to_all(pieces, ("xh", "c"), split_axis=0, concat_axis=0, tiled=True)
    fields = filtered_and_applied(
        own.astype(jnp.int32).reshape(1), mixed, boundary.reshape(4, 2, 4, PLANE)
    )
    shares = fields.reshape(4, SHARES, SHARE).transpose(1, 0, 2)
    shares = lax.all_to_all(shares, "z", split_axis=0, concat_axis=0, tiled=True)
    cols = shares.reshape(4 * SHARES, SHARE)
    cols = lax.all_to_all(
        jnp.broadcast_to(cols[None], (4, 4 * SHARES, SHARE)), "y", split_axis=0, concat_axis=0, tiled=True
    )
    rows = shares[:, :2].reshape(2 * SHARES, SHARE)
    rows = lax.all_gather(rows, ("xl", "xh"), axis=0, tiled=True)
    other = lax.ppermute(rows, "c", [(0, 1), (1, 0)])
    core = lax.axis_index("c").astype(jnp.int32).reshape(1)
    partial = block_product(core, rows, other, cols.reshape(256, SHARE))
    parts = lax.all_to_all(partial, ("z", "xl", "xh", "c"), split_axis=0, concat_axis=0, tiled=True)
    correlation, projected = finish(parts.reshape(16, 8, 8, 64))
    return correlation, projected


def solution(mesh):
    split = Mesh(mesh.devices.reshape(16, 4, 2, 2, 2), ("z", "y", "xl", "xh", "c"))
    band, domain = ("z", "y", "xl"), ("xh", "c")
    return jax.shard_map(
        per_device,
        mesh=split,
        in_specs=(P(band, domain, None), P(band, None, None), P(domain, None)),
        out_specs=(P(band, domain), P(band, domain)),
        check_vma=False,
    )
```

```python
import jax
import jax.numpy as jnp
from jax import lax
from jax.experimental import pallas as pl
from jax.experimental.pallas import tpu as pltpu
from jax.sharding import Mesh, PartitionSpec as P

NX = 160
NY = 32
NZ = 8
PLANE = NX * NY
DEGREE = 4
PAD = 384
SPAN = 640
CHUNKS = PLANE // SPAN
SHARES = 16
SHARE = NZ * PLANE // SHARES

filter_center = 5.5
filter_radius = 4.5


def filter_kernel(which, mixed_ref, rim_ref, out_ref, one, two, rim_term, pot):
    row = lax.broadcasted_iota(jnp.int32, (NZ, SPAN), 0)
    x = lax.rem(lax.broadcasted_iota(jnp.int32, (NZ, SPAN), 1), NX)
    zero = jnp.zeros((NZ, SPAN), jnp.float32)
    below_1 = jnp.where(row >= 1, zero + 16.0, zero)
    above_1 = jnp.where(row <= NZ - 2, zero + 16.0, zero)
    below_2 = jnp.where(row >= 2, zero + 1.0, zero)
    above_2 = jnp.where(row <= NZ - 3, zero + 1.0, zero)
    first, last = x == 0, x == NX - 1
    first_two, last_two = x <= 1, x >= NX - 2

    def wrap(ref, orb):
        ref[orb, :, 0:PAD] = ref[orb, :, PLANE : PLANE + PAD]
        ref[orb, :, PAD + PLANE : 2 * PAD + PLANE] = ref[orb, :, PAD : 2 * PAD]

    pot[...] = jnp.concatenate([mixed_ref[s, 2] for s in range(4)], axis=0).astype(jnp.float32)
    for orb in range(2):
        planes = [mixed_ref[s, orb] for s in range(4)]
        one[orb, :, PAD : PAD + PLANE] = jnp.concatenate(planes, axis=0).astype(jnp.float32)
        wrap(one, orb)
        rim = rim_ref[which[0], orb].astype(jnp.float32)
        low_far, low, high, high_far = (rim[k : k + 1] for k in range(4))
        rim_term[orb] = jnp.concatenate(
            [16.0 * low - low_far, -low, jnp.zeros((4, PLANE), jnp.float32), -high, 16.0 * high - high_far],
            axis=0,
        )

    def apply_ham(ref, orb, at):
        window = ref[orb, :, pl.ds(at, SPAN + 2 * PAD)]
        width = SPAN + 2 * PAD

        def cells(shift):
            return pltpu.roll(window, (-shift) % width, 1)[:, PAD : PAD + SPAN]

        middle = window[:, PAD : PAD + SPAN]
        near = jnp.where(first, cells(NX - 1), cells(-1)) + jnp.where(last, cells(1 - NX), cells(1))
        near = near + (cells(NX) + cells(-NX))
        far = jnp.where(first_two, cells(NX - 2), cells(-2)) + jnp.where(
            last_two, cells(2 - NX), cells(2)
        )
        far = far + (cells(2 * NX) + cells(-2 * NX))
        z_near = below_1 * pltpu.roll(middle, 1, 0) + above_1 * pltpu.roll(middle, NZ - 1, 0)
        z_far = below_2 * pltpu.roll(middle, 2, 0) + above_2 * pltpu.roll(middle, NZ - 2, 0)
        total = (16.0 * near - far) + (z_near - z_far) - 90.0 * middle
        total = total + rim_term[orb, :, pl.ds(at, SPAN)]
        return total * (-0.5 / 12.0) + pot[:, pl.ds(at, SPAN)] * middle, middle

    current, earlier = one, two
    for step in range(DEGREE):

        def body(chunk, carry, step=step, current=current, earlier=earlier):
            at = chunk * SPAN
            for orb in range(2):
                with_h, middle = apply_ham(current, orb, at)
                following = (with_h - filter_center * middle) * (1.0 / filter_radius)
                place = (orb, slice(None), pl.ds(at + PAD, SPAN))
                if step > 0:
                    following = 2.0 * following - earlier[place]
                earlier[place] = following.astype(jnp.bfloat16).astype(jnp.float32)
            return carry

        for chunk in range(CHUNKS):
            body(chunk, 0)
        for orb in range(2):
            wrap(earlier, orb)
        current, earlier = earlier, current

    def last_body(chunk, carry):
        at = chunk * SPAN
        for orb in range(2):
            with_h, middle = apply_ham(current, orb, at)
            out_ref[orb, :, pl.ds(at, SPAN)] = middle.astype(jnp.bfloat16)
            out_ref[2 + orb, :, pl.ds(at, SPAN)] = with_h.astype(jnp.bfloat16)
        return carry

    for chunk in range(CHUNKS):
        last_body(chunk, 0)


def filtered_and_applied(which, mixed, boundary):
    whole = pl.BlockSpec(memory_space=pltpu.VMEM)
    return pl.pallas_call(
        filter_kernel,
        in_specs=[pl.BlockSpec(memory_space=pltpu.SMEM), whole, whole],
        out_specs=whole,
        out_shape=jax.ShapeDtypeStruct((4, NZ, PLANE), jnp.bfloat16),
        scratch_shapes=[
            pltpu.VMEM((2, NZ, PLANE + 2 * PAD), jnp.float32),
            pltpu.VMEM((2, NZ, PLANE + 2 * PAD), jnp.float32),
            pltpu.VMEM((2, NZ, PLANE), jnp.float32),
            pltpu.VMEM((NZ, PLANE), jnp.float32),
        ],
        compiler_params=pltpu.CompilerParams(vmem_limit_bytes=24 * 1024 * 1024),
        name="chebyshev_filter",
    )(which, mixed, boundary)


def swapped(values):
    return pltpu.roll(values, 64, 1)


def product_kernel(core_ref, own_ref, other_ref, cols_ref, out_ref, blocks):
    core = core_ref[0]
    cols = jnp.concatenate(
        [cols_ref[y, 16 * zh : 16 * zh + 16, :] for zh in range(4) for y in range(4)], axis=0
    )
    left = lax.broadcasted_iota(jnp.int32, (64, 128), 1) < 64
    for rows_ref, place in ((own_ref, core), (other_ref, 1 - core)):
        block = lax.dot_general(
            rows_ref[...], cols, (((1,), (1,)), ((), ())), preferred_element_type=jnp.float32
        )
        for pair in range(2):
            low = block[:64, 128 * pair : 128 * pair + 128]
            high = block[64:, 128 * pair : 128 * pair + 128]
            blocks[place, 2 * pair] = jnp.where(left, low, swapped(high))
            blocks[place, 2 * pair + 1] = jnp.where(left, swapped(low), high)
    for z in range(16):
        for xl in range(2):
            for zh in range(4):
                for c in range(2):
                    out_ref[(z * 2 + xl) * 4 + zh, 2 * c : 2 * c + 2, :] = blocks[
                        c, zh, xl * 32 + z * 2 : xl * 32 + z * 2 + 2, :
                    ]


def block_product(core, own, other, cols):
    whole = pl.BlockSpec(memory_space=pltpu.VMEM)
    return pl.pallas_call(
        product_kernel,
        in_specs=[pl.BlockSpec(memory_space=pltpu.SMEM), whole, whole, whole],
        out_specs=whole,
        out_shape=jax.ShapeDtypeStruct((128, 4, 128), jnp.float32),
        scratch_shapes=[pltpu.VMEM((2, 4, 64, 128), jnp.float32)],
        compiler_params=pltpu.CompilerParams(vmem_limit_bytes=24 * 1024 * 1024),
        name="block_product",
    )(core, own, other, cols)


def finish_kernel(parts_ref, correlation_ref, projected_ref):
    left = lax.broadcasted_iota(jnp.int32, (4, 128), 1) < 64
    pieces = []
    for pair in range(4):
        one, two = parts_ref[2 * pair], parts_ref[2 * pair + 1]
        for k in range(1, 16):
            one = one + parts_ref[8 * k + 2 * pair]
            two = two + parts_ref[8 * k + 2 * pair + 1]
        low = jnp.where(left, one, swapped(two))
        high = jnp.where(left, swapped(one), two)
        pieces.append(jnp.concatenate([low, high], axis=0))
    given = jnp.concatenate(pieces, axis=1) * (1.0 / (NZ * PLANE))
    at = lax.broadcasted_iota(jnp.int32, (1, 512), 1)

    def field(shift, count):
        return lax.shift_right_logical(at, shift) & (count - 1)

    group = field(3, 2) * 4 + field(1, 4)
    source = group * 64 + field(4, 4) * 16 + field(6, 4) * 4 + field(8, 2) * 2 + field(0, 2)
    hot = jnp.where(lax.broadcasted_iota(jnp.int32, (512, 512), 0) == source, 1.0, 0.0)
    top = given.astype(jnp.bfloat16)
    rest = given - top.astype(jnp.float32)
    middle = rest.astype(jnp.bfloat16)
    last = (rest - middle.astype(jnp.float32)).astype(jnp.bfloat16)
    split = jnp.concatenate(
        [top.astype(jnp.float32), middle.astype(jnp.float32), last.astype(jnp.float32)], axis=0
    )
    placed = jnp.dot(
        split.astype(jnp.bfloat16), hot.astype(jnp.bfloat16), preferred_element_type=jnp.float32
    )
    placed = (placed[16:] + placed[8:16]) + placed[:8]
    correlation_ref[...] = placed[:, :256]
    projected_ref[...] = placed[:, 256:]


def finish(parts):
    shape = jax.ShapeDtypeStruct((8, 256), jnp.float32)
    whole = pl.BlockSpec(memory_space=pltpu.VMEM)
    return pl.pallas_call(
        finish_kernel,
        in_specs=[whole],
        out_specs=[whole, whole],
        out_shape=[shape, shape],
        name="finish",
    )(parts)


def per_device(orbitals, boundary, potential):
    own = lax.axis_index("xh") * 2 + lax.axis_index("c")
    pieces = jnp.concatenate(
        [orbitals.reshape(4, 2, 2, PLANE), jnp.broadcast_to(potential, (4, 1, 2, PLANE))], axis=1
    )
    mixed = lax.all_to_all(pieces, ("xh", "c"), split_axis=0, concat_axis=0, tiled=True)
    fields = filtered_and_applied(
        own.astype(jnp.int32).reshape(1), mixed, boundary.reshape(4, 2, 4, PLANE)
    )
    shares = fields.reshape(4, SHARES, SHARE).transpose(1, 0, 2)
    shares = lax.all_to_all(shares, "z", split_axis=0, concat_axis=0, tiled=True)
    cols = shares.reshape(4 * SHARES, SHARE)
    cols = lax.all_to_all(
        jnp.broadcast_to(cols[None], (4, 4 * SHARES, SHARE)), "y", split_axis=0, concat_axis=0, tiled=True
    )
    rows = shares[:, :2].reshape(2 * SHARES, SHARE)
    rows = lax.all_gather(rows, ("xh", "xl"), axis=0, tiled=True)
    other = lax.ppermute(rows, "c", [(0, 1), (1, 0)])
    core = lax.axis_index("c").astype(jnp.int32).reshape(1)
    partial = block_product(core, rows, other, cols)
    parts = lax.all_to_all(partial, ("z", "xl", "xh", "c"), split_axis=0, concat_axis=0, tiled=True)
    return tuple(finish(parts))


def solution(mesh):
    split = Mesh(mesh.devices.reshape(16, 4, 2, 2, 2), ("z", "y", "xl", "xh", "c"))
    band, domain = ("z", "y", "xl"), ("xh", "c")
    return jax.shard_map(
        per_device,
        mesh=split,
        in_specs=(P(band, domain, None), P(band, None, None), P(domain, None)),
        out_specs=(P(band, domain), P(band, domain)),
        check_vma=False,
    )
```

```python
import jax
import jax.numpy as jnp
from jax import lax
from jax.experimental import pallas as pl
from jax.experimental.pallas import tpu as pltpu
from jax.sharding import Mesh, PartitionSpec as P

NX = 160
NY = 32
NZ = 8
PLANE = NX * NY
DEGREE = 4
PAD = 384
SPAN = 640
CHUNKS = PLANE // SPAN
SHARES = 16
SHARE = NZ * PLANE // SHARES

filter_center = 5.5
filter_radius = 4.5


def prepare_kernel(which, rim_ref, rim_term, hot_ref):
    for orb in range(2):
        rim = rim_ref[which[0], orb].astype(jnp.float32)
        low_far, low, high, high_far = (rim[k : k + 1] for k in range(4))
        rim_term[orb] = jnp.concatenate(
            [16.0 * low - low_far, -low, jnp.zeros((4, PLANE), jnp.float32), -high, 16.0 * high - high_far],
            axis=0,
        )
    at = lax.broadcasted_iota(jnp.int32, (1, 512), 1)

    def field(shift, count):
        return lax.shift_right_logical(at, shift) & (count - 1)

    group = field(3, 2) * 4 + field(1, 4)
    source = group * 64 + field(4, 4) * 16 + field(6, 4) * 4 + field(8, 2) * 2 + field(0, 2)
    hot = jnp.where(lax.broadcasted_iota(jnp.int32, (512, 512), 0) == source, 1.0, 0.0)
    hot_ref[...] = hot.astype(jnp.bfloat16)


def prepared(which, boundary):
    whole = pl.BlockSpec(memory_space=pltpu.VMEM)
    return pl.pallas_call(
        prepare_kernel,
        in_specs=[pl.BlockSpec(memory_space=pltpu.SMEM), whole],
        out_specs=[whole, whole],
        out_shape=[
            jax.ShapeDtypeStruct((2, NZ, PLANE), jnp.float32),
            jax.ShapeDtypeStruct((512, 512), jnp.bfloat16),
        ],
        name="prepare",
    )(which, boundary)


def filter_kernel(mixed_ref, rim_term, out_ref, one, two, pot):
    row = lax.broadcasted_iota(jnp.int32, (NZ, SPAN), 0)
    zero = jnp.zeros((NZ, SPAN), jnp.float32)
    below_1 = jnp.where(row >= 1, zero + 16.0, zero)
    above_1 = jnp.where(row <= NZ - 2, zero + 16.0, zero)
    below_2 = jnp.where(row >= 2, zero + 1.0, zero)
    above_2 = jnp.where(row <= NZ - 3, zero + 1.0, zero)
    width = SPAN + 2 * PAD
    x = lax.rem(lax.broadcasted_iota(jnp.int32, (NZ, width), 1) + (3 * NX - PAD), NX)
    first, last = x == 0, x == NX - 1
    first_two, last_two = x <= 1, x >= NX - 2

    def wrap(ref, orb):
        ref[orb, :, 0:PAD] = ref[orb, :, PLANE : PLANE + PAD]
        ref[orb, :, PAD + PLANE : 2 * PAD + PLANE] = ref[orb, :, PAD : 2 * PAD]

    pot[...] = jnp.concatenate([mixed_ref[s, 2] for s in range(4)], axis=0).astype(jnp.float32)
    for orb in range(2):
        planes = [mixed_ref[s, orb] for s in range(4)]
        one[orb, :, PAD : PAD + PLANE] = jnp.concatenate(planes, axis=0).astype(jnp.float32)
        wrap(one, orb)

    def apply_ham(ref, orb, at):
        window = ref[orb, :, pl.ds(at, SPAN + 2 * PAD)]

        def moved(values, shift):
            return pltpu.roll(values, (-shift) % width, 1)

        def inner(values):
            return values[:, PAD : PAD + SPAN]

        middle = inner(window)
        up, down = moved(window, NX), moved(window, -NX)
        near = inner(moved(jnp.where(last, up, window), -1))
        near = near + inner(moved(jnp.where(first, down, window), 1))
        near = near + (inner(up) + inner(down))
        far = inner(moved(jnp.where(last_two, up, window), -2))
        far = far + inner(moved(jnp.where(first_two, down, window), 2))
        far = far + (inner(moved(window, 2 * NX)) + inner(moved(window, -2 * NX)))
        z_near = below_1 * pltpu.roll(middle, 1, 0) + above_1 * pltpu.roll(middle, NZ - 1, 0)
        z_far = below_2 * pltpu.roll(middle, 2, 0) + above_2 * pltpu.roll(middle, NZ - 2, 0)
        total = (16.0 * near - far) + (z_near - z_far) - 90.0 * middle
        total = total + rim_term[orb, :, pl.ds(at, SPAN)]
        return total * (-0.5 / 12.0) + pot[:, pl.ds(at, SPAN)] * middle, middle

    current, earlier = one, two
    for step in range(DEGREE):

        def body(chunk, carry, step=step, current=current, earlier=earlier):
            at = chunk * SPAN
            for orb in range(2):
                with_h, middle = apply_ham(current, orb, at)
                following = (with_h - filter_center * middle) * (1.0 / filter_radius)
                place = (orb, slice(None), pl.ds(at + PAD, SPAN))
                if step > 0:
                    following = 2.0 * following - earlier[place]
                earlier[place] = following.astype(jnp.bfloat16).astype(jnp.float32)
            return carry

        for chunk in range(CHUNKS):
            body(chunk, 0)
        for orb in range(2):
            wrap(earlier, orb)
        current, earlier = earlier, current

    def last_body(chunk, carry):
        at = chunk * SPAN
        for orb in range(2):
            with_h, middle = apply_ham(current, orb, at)
            out_ref[orb, :, pl.ds(at, SPAN)] = middle.astype(jnp.bfloat16)
            out_ref[2 + orb, :, pl.ds(at, SPAN)] = with_h.astype(jnp.bfloat16)
        return carry

    for chunk in range(CHUNKS):
        last_body(chunk, 0)


def filtered_and_applied(mixed, rim_term):
    whole = pl.BlockSpec(memory_space=pltpu.VMEM)
    return pl.pallas_call(
        filter_kernel,
        in_specs=[whole, whole],
        out_specs=whole,
        out_shape=jax.ShapeDtypeStruct((4, NZ, PLANE), jnp.bfloat16),
        scratch_shapes=[
            pltpu.VMEM((2, NZ, PLANE + 2 * PAD), jnp.float32),
            pltpu.VMEM((2, NZ, PLANE + 2 * PAD), jnp.float32),
            pltpu.VMEM((NZ, PLANE), jnp.float32),
        ],
        compiler_params=pltpu.CompilerParams(vmem_limit_bytes=24 * 1024 * 1024),
        name="chebyshev_filter",
    )(mixed, rim_term)


def swapped(values):
    return pltpu.roll(values, 64, 1)


def product_kernel(core_ref, own_ref, other_ref, cols_ref, out_ref, blocks):
    core = core_ref[0]
    cols = jnp.concatenate(
        [cols_ref[y, 16 * zh : 16 * zh + 16, :] for zh in range(4) for y in range(4)], axis=0
    )
    left = lax.broadcasted_iota(jnp.int32, (64, 128), 1) < 64
    for rows_ref, place in ((own_ref, core), (other_ref, 1 - core)):
        block = lax.dot_general(
            rows_ref[...], cols, (((1,), (1,)), ((), ())), preferred_element_type=jnp.float32
        )
        for pair in range(2):
            low = block[:64, 128 * pair : 128 * pair + 128]
            high = block[64:, 128 * pair : 128 * pair + 128]
            blocks[place, 2 * pair] = jnp.where(left, low, swapped(high))
            blocks[place, 2 * pair + 1] = jnp.where(left, swapped(low), high)
    for z in range(16):
        for xl in range(2):
            for zh in range(4):
                for c in range(2):
                    out_ref[(z * 2 + xl) * 4 + zh, 2 * c : 2 * c + 2, :] = blocks[
                        c, zh, xl * 32 + z * 2 : xl * 32 + z * 2 + 2, :
                    ]


def block_product(core, own, other, cols):
    whole = pl.BlockSpec(memory_space=pltpu.VMEM)
    return pl.pallas_call(
        product_kernel,
        in_specs=[pl.BlockSpec(memory_space=pltpu.SMEM), whole, whole, whole],
        out_specs=whole,
        out_shape=jax.ShapeDtypeStruct((128, 4, 128), jnp.float32),
        scratch_shapes=[pltpu.VMEM((2, 4, 64, 128), jnp.float32)],
        compiler_params=pltpu.CompilerParams(vmem_limit_bytes=24 * 1024 * 1024),
        name="block_product",
    )(core, own, other, cols)


def finish_kernel(parts_ref, hot_ref, correlation_ref, projected_ref):
    left = lax.broadcasted_iota(jnp.int32, (4, 128), 1) < 64
    pieces = []
    for pair in range(4):
        one, two = parts_ref[2 * pair], parts_ref[2 * pair + 1]
        for k in range(1, 16):
            one = one + parts_ref[8 * k + 2 * pair]
            two = two + parts_ref[8 * k + 2 * pair + 1]
        low = jnp.where(left, one, swapped(two))
        high = jnp.where(left, swapped(one), two)
        pieces.append(jnp.concatenate([low, high], axis=0))
    given = jnp.concatenate(pieces, axis=1) * (1.0 / (NZ * PLANE))
    top = given.astype(jnp.bfloat16)
    rest = given - top.astype(jnp.float32)
    middle = rest.astype(jnp.bfloat16)
    last = (rest - middle.astype(jnp.float32)).astype(jnp.bfloat16)
    split = jnp.concatenate(
        [top.astype(jnp.float32), middle.astype(jnp.float32), last.astype(jnp.float32)], axis=0
    )
    placed = jnp.dot(split.astype(jnp.bfloat16), hot_ref[...], preferred_element_type=jnp.float32)
    placed = (placed[16:] + placed[8:16]) + placed[:8]
    correlation_ref[...] = placed[:, :256]
    projected_ref[...] = placed[:, 256:]


def finish(parts, hot):
    shape = jax.ShapeDtypeStruct((8, 256), jnp.float32)
    whole = pl.BlockSpec(memory_space=pltpu.VMEM)
    return pl.pallas_call(
        finish_kernel,
        in_specs=[whole, whole],
        out_specs=[whole, whole],
        out_shape=[shape, shape],
        name="finish",
    )(parts, hot)


def pieces_kernel(orbitals_ref, potential_ref, out_ref, sems):
    copies = [pltpu.make_async_copy(orbitals_ref, out_ref.at[:, 0:2], sems.at[0])]
    for k in range(4):
        copies.append(pltpu.make_async_copy(potential_ref, out_ref.at[k, 2], sems.at[1 + k]))
    for copy in copies:
        copy.start()
    for copy in copies:
        copy.wait()


def pieces_of(orbitals, potential):
    anywhere = pl.BlockSpec(memory_space=pl.ANY)
    return pl.pallas_call(
        pieces_kernel,
        in_specs=[anywhere, anywhere],
        out_specs=anywhere,
        out_shape=jax.ShapeDtypeStruct((4, 3, 2, PLANE), jnp.bfloat16),
        scratch_shapes=[pltpu.SemaphoreType.DMA((5,))],
        name="pieces",
    )(orbitals, potential)


def per_device(orbitals, boundary, potential):
    own = lax.axis_index("xh") * 2 + lax.axis_index("c")
    pieces = pieces_of(orbitals.reshape(4, 2, 2, PLANE), potential)
    mixed = lax.all_to_all(pieces, ("xh", "c"), split_axis=0, concat_axis=0, tiled=True)
    rim_term, hot = prepared(own.astype(jnp.int32).reshape(1), boundary.reshape(4, 2, 4, PLANE))
    fields = filtered_and_applied(mixed, rim_term)
    shares = fields.reshape(4, SHARES, SHARE).transpose(1, 0, 2)
    shares = lax.all_to_all(shares, "z", split_axis=0, concat_axis=0, tiled=True)
    cols = shares.reshape(4 * SHARES, SHARE)
    cols = lax.all_to_all(
        jnp.broadcast_to(cols[None], (4, 4 * SHARES, SHARE)), "y", split_axis=0, concat_axis=0, tiled=True
    )
    rows = shares[:, :2].reshape(2 * SHARES, SHARE)
    rows = lax.all_gather(rows, ("xh", "xl"), axis=0, tiled=True)
    other = lax.ppermute(rows, "c", [(0, 1), (1, 0)])
    core = lax.axis_index("c").astype(jnp.int32).reshape(1)
    partial = block_product(core, rows, other, cols)
    parts = lax.all_to_all(partial, ("z", "xl", "xh", "c"), split_axis=0, concat_axis=0, tiled=True)
    return tuple(finish(parts, hot))


def solution(mesh):
    split = Mesh(mesh.devices.reshape(16, 4, 2, 2, 2), ("z", "y", "xl", "xh", "c"))
    band, domain = ("z", "y", "xl"), ("xh", "c")
    return jax.shard_map(
        per_device,
        mesh=split,
        in_specs=(P(band, domain, None), P(band, None, None), P(domain, None)),
        out_specs=(P(band, domain), P(band, domain)),
        check_vma=False,
    )
```

```python
import jax
import jax.numpy as jnp
from jax import lax
from jax.experimental import pallas as pl
from jax.experimental.pallas import tpu as pltpu
from jax.sharding import Mesh, PartitionSpec as P

NX = 160
NY = 32
NZ = 8
PLANE = NX * NY
DEGREE = 4
PAD = 384
SPAN = 640
CHUNKS = PLANE // SPAN
SHARES = 16
SHARE = NZ * PLANE // SHARES

filter_center = 5.5
filter_radius = 4.5


def filter_kernel(mixed_ref, rim_ref, out_ref, one, two, rim_term, pot):
    row = lax.broadcasted_iota(jnp.int32, (NZ, SPAN), 0)
    x = lax.rem(lax.broadcasted_iota(jnp.int32, (NZ, SPAN), 1), NX)
    zero = jnp.zeros((NZ, SPAN), jnp.float32)
    below_1 = jnp.where(row >= 1, zero + 16.0, zero)
    above_1 = jnp.where(row <= NZ - 2, zero + 16.0, zero)
    below_2 = jnp.where(row >= 2, zero + 1.0, zero)
    above_2 = jnp.where(row <= NZ - 3, zero + 1.0, zero)
    first, last = x == 0, x == NX - 1
    first_two, last_two = x <= 1, x >= NX - 2

    def wrap(ref, orb):
        ref[orb, :, 0:PAD] = ref[orb, :, PLANE : PLANE + PAD]
        ref[orb, :, PAD + PLANE : 2 * PAD + PLANE] = ref[orb, :, PAD : 2 * PAD]

    pot[...] = jnp.concatenate([mixed_ref[s, 2] for s in range(4)], axis=0).astype(jnp.float32)
    for orb in range(2):
        planes = [mixed_ref[s, orb] for s in range(4)]
        one[orb, :, PAD : PAD + PLANE] = jnp.concatenate(planes, axis=0).astype(jnp.float32)
        wrap(one, orb)
        rim = rim_ref[orb].astype(jnp.float32)
        low_far, low, high, high_far = (rim[k : k + 1] for k in range(4))
        rim_term[orb] = jnp.concatenate(
            [16.0 * low - low_far, -low, jnp.zeros((4, PLANE), jnp.float32), -high, 16.0 * high - high_far],
            axis=0,
        )

    def apply_ham(ref, orb, at):
        window = ref[orb, :, pl.ds(at, SPAN + 2 * PAD)]
        width = SPAN + 2 * PAD

        def cells(shift):
            return pltpu.roll(window, (-shift) % width, 1)[:, PAD : PAD + SPAN]

        middle = window[:, PAD : PAD + SPAN]
        near = jnp.where(first, cells(NX - 1), cells(-1)) + jnp.where(last, cells(1 - NX), cells(1))
        near = near + (cells(NX) + cells(-NX))
        far = jnp.where(first_two, cells(NX - 2), cells(-2)) + jnp.where(
            last_two, cells(2 - NX), cells(2)
        )
        far = far + (cells(2 * NX) + cells(-2 * NX))
        z_near = below_1 * pltpu.roll(middle, 1, 0) + above_1 * pltpu.roll(middle, NZ - 1, 0)
        z_far = below_2 * pltpu.roll(middle, 2, 0) + above_2 * pltpu.roll(middle, NZ - 2, 0)
        total = (16.0 * near - far) + (z_near - z_far) - 90.0 * middle
        total = total + rim_term[orb, :, pl.ds(at, SPAN)]
        return total * (-0.5 / 12.0) + pot[:, pl.ds(at, SPAN)] * middle, middle

    current, earlier = one, two
    for step in range(DEGREE):

        def body(chunk, carry, step=step, current=current, earlier=earlier):
            at = chunk * SPAN
            for orb in range(2):
                with_h, middle = apply_ham(current, orb, at)
                following = (with_h - filter_center * middle) * (1.0 / filter_radius)
                place = (orb, slice(None), pl.ds(at + PAD, SPAN))
                if step > 0:
                    following = 2.0 * following - earlier[place]
                earlier[place] = following.astype(jnp.bfloat16).astype(jnp.float32)
            return carry

        for chunk in range(CHUNKS):
            body(chunk, 0)
        for orb in range(2):
            wrap(earlier, orb)
        current, earlier = earlier, current

    def last_body(chunk, carry):
        at = chunk * SPAN
        for orb in range(2):
            with_h, middle = apply_ham(current, orb, at)
            out_ref[orb, :, pl.ds(at, SPAN)] = middle.astype(jnp.bfloat16)
            out_ref[2 + orb, :, pl.ds(at, SPAN)] = with_h.astype(jnp.bfloat16)
        return carry

    for chunk in range(CHUNKS):
        last_body(chunk, 0)


def filtered_and_applied(mixed, rim):
    whole = pl.BlockSpec(memory_space=pltpu.VMEM)
    return pl.pallas_call(
        filter_kernel,
        in_specs=[whole, whole],
        out_specs=whole,
        out_shape=jax.ShapeDtypeStruct((4, NZ, PLANE), jnp.bfloat16),
        scratch_shapes=[
            pltpu.VMEM((2, NZ, PLANE + 2 * PAD), jnp.float32),
            pltpu.VMEM((2, NZ, PLANE + 2 * PAD), jnp.float32),
            pltpu.VMEM((2, NZ, PLANE), jnp.float32),
            pltpu.VMEM((NZ, PLANE), jnp.float32),
        ],
        compiler_params=pltpu.CompilerParams(vmem_limit_bytes=24 * 1024 * 1024),
        name="chebyshev_filter",
    )(mixed, rim)


def swapped(values):
    return pltpu.roll(values, 64, 1)


def product_kernel(core_ref, own_ref, other_ref, cols_ref, out_ref, blocks):
    core = core_ref[0]
    cols = jnp.concatenate(
        [cols_ref[y, 16 * zh : 16 * zh + 16, :] for zh in range(4) for y in range(4)], axis=0
    )
    left = lax.broadcasted_iota(jnp.int32, (64, 128), 1) < 64
    for rows_ref, place in ((own_ref, core), (other_ref, 1 - core)):
        block = lax.dot_general(
            rows_ref[...], cols, (((1,), (1,)), ((), ())), preferred_element_type=jnp.float32
        )
        for pair in range(2):
            low = block[:64, 128 * pair : 128 * pair + 128]
            high = block[64:, 128 * pair : 128 * pair + 128]
            blocks[place, 2 * pair] = jnp.where(left, low, swapped(high))
            blocks[place, 2 * pair + 1] = jnp.where(left, swapped(low), high)
    for z in range(16):
        for xl in range(2):
            for zh in range(4):
                for c in range(2):
                    out_ref[(z * 2 + xl) * 4 + zh, 2 * c : 2 * c + 2, :] = blocks[
                        c, zh, xl * 32 + z * 2 : xl * 32 + z * 2 + 2, :
                    ]


def block_product(core, own, other, cols):
    whole = pl.BlockSpec(memory_space=pltpu.VMEM)
    return pl.pallas_call(
        product_kernel,
        in_specs=[pl.BlockSpec(memory_space=pltpu.SMEM), whole, whole, whole],
        out_specs=whole,
        out_shape=jax.ShapeDtypeStruct((128, 4, 128), jnp.float32),
        scratch_shapes=[pltpu.VMEM((2, 4, 64, 128), jnp.float32)],
        compiler_params=pltpu.CompilerParams(vmem_limit_bytes=24 * 1024 * 1024),
        name="block_product",
    )(core, own, other, cols)


def finish_kernel(parts_ref, correlation_ref, projected_ref):
    left = lax.broadcasted_iota(jnp.int32, (4, 128), 1) < 64
    pieces = []
    for pair in range(4):
        one, two = parts_ref[2 * pair], parts_ref[2 * pair + 1]
        for k in range(1, 16):
            one = one + parts_ref[8 * k + 2 * pair]
            two = two + parts_ref[8 * k + 2 * pair + 1]
        low = jnp.where(left, one, swapped(two))
        high = jnp.where(left, swapped(one), two)
        pieces.append(jnp.concatenate([low, high], axis=0))
    given = jnp.concatenate(pieces, axis=1) * (1.0 / (NZ * PLANE))
    at = lax.broadcasted_iota(jnp.int32, (1, 512), 1)

    def field(shift, count):
        return lax.shift_right_logical(at, shift) & (count - 1)

    group = field(3, 2) * 4 + field(1, 4)
    source = group * 64 + field(4, 4) * 16 + field(6, 4) * 4 + field(8, 2) * 2 + field(0, 2)
    hot = jnp.where(lax.broadcasted_iota(jnp.int32, (512, 512), 0) == source, 1.0, 0.0)
    top = given.astype(jnp.bfloat16)
    rest = given - top.astype(jnp.float32)
    middle = rest.astype(jnp.bfloat16)
    last = (rest - middle.astype(jnp.float32)).astype(jnp.bfloat16)
    split = jnp.concatenate(
        [top.astype(jnp.float32), middle.astype(jnp.float32), last.astype(jnp.float32)], axis=0
    )
    placed = jnp.dot(
        split.astype(jnp.bfloat16), hot.astype(jnp.bfloat16), preferred_element_type=jnp.float32
    )
    placed = (placed[16:] + placed[8:16]) + placed[:8]
    correlation_ref[...] = placed[:, :256]
    projected_ref[...] = placed[:, 256:]


def finish(parts):
    shape = jax.ShapeDtypeStruct((8, 256), jnp.float32)
    whole = pl.BlockSpec(memory_space=pltpu.VMEM)
    return pl.pallas_call(
        finish_kernel,
        in_specs=[whole],
        out_specs=[whole, whole],
        out_shape=[shape, shape],
        compiler_params=pltpu.CompilerParams(vmem_limit_bytes=8 * 1024 * 1024),
        name="finish",
    )(parts)


def pieces_kernel(which, orbitals_ref, potential_ref, rim_ref, out_ref, own_rim_ref, sems):
    copies = [
        pltpu.make_async_copy(orbitals_ref, out_ref.at[:, 0:2], sems.at[0]),
        pltpu.make_async_copy(rim_ref.at[which[0]], own_rim_ref, sems.at[1]),
    ]
    for k in range(4):
        copies.append(pltpu.make_async_copy(potential_ref, out_ref.at[k, 2], sems.at[2 + k]))
    for copy in copies:
        copy.start()
    for copy in copies:
        copy.wait()


def pieces_of(which, orbitals, potential, boundary):
    anywhere = pl.BlockSpec(memory_space=pl.ANY)
    whole = pl.BlockSpec(memory_space=pltpu.VMEM)
    return pl.pallas_call(
        pieces_kernel,
        in_specs=[pl.BlockSpec(memory_space=pltpu.SMEM), anywhere, anywhere, anywhere],
        out_specs=[whole, whole],
        out_shape=[
            jax.ShapeDtypeStruct((4, 3, 2, PLANE), jnp.bfloat16),
            jax.ShapeDtypeStruct((2, 4, PLANE), jnp.bfloat16),
        ],
        scratch_shapes=[pltpu.SemaphoreType.DMA((6,))],
        compiler_params=pltpu.CompilerParams(vmem_limit_bytes=56 * 1024 * 1024),
        name="pieces",
    )(which, orbitals, potential, boundary)


def per_device(orbitals, boundary, potential):
    own = lax.axis_index("xh") * 2 + lax.axis_index("c")
    pieces, own_rim = pieces_of(
        own.astype(jnp.int32).reshape(1),
        orbitals.reshape(4, 2, 2, PLANE),
        potential,
        boundary.reshape(4, 2, 4, PLANE),
    )
    mixed = lax.all_to_all(pieces, ("xh", "c"), split_axis=0, concat_axis=0, tiled=True)
    fields = filtered_and_applied(mixed, own_rim)
    shares = fields.reshape(4, SHARES, SHARE).transpose(1, 0, 2)
    shares = lax.all_to_all(shares, "z", split_axis=0, concat_axis=0, tiled=True)
    cols = shares.reshape(4 * SHARES, SHARE)
    cols = lax.all_to_all(
        jnp.broadcast_to(cols[None], (4, 4 * SHARES, SHARE)), "y", split_axis=0, concat_axis=0, tiled=True
    )
    rows = shares[:, :2].reshape(2 * SHARES, SHARE)
    rows = lax.all_gather(rows, ("xh", "xl"), axis=0, tiled=True)
    other = lax.ppermute(rows, "c", [(0, 1), (1, 0)])
    core = lax.axis_index("c").astype(jnp.int32).reshape(1)
    partial = block_product(core, rows, other, cols)
    parts = lax.all_to_all(partial, ("z", "xl", "xh", "c"), split_axis=0, concat_axis=0, tiled=True)
    return tuple(finish(parts))


def solution(mesh):
    split = Mesh(mesh.devices.reshape(16, 4, 2, 2, 2), ("z", "y", "xl", "xh", "c"))
    band, domain = ("z", "y", "xl"), ("xh", "c")
    return jax.shard_map(
        per_device,
        mesh=split,
        in_specs=(P(band, domain, None), P(band, None, None), P(domain, None)),
        out_specs=(P(band, domain), P(band, domain)),
        check_vma=False,
    )
```

```python
import jax
import jax.numpy as jnp
from jax import lax
from jax.experimental import pallas as pl
from jax.experimental.pallas import tpu as pltpu
from jax.sharding import Mesh, PartitionSpec as P

NX = 160
NY = 32
NZ = 8
PLANE = NX * NY
DEGREE = 4
PAD = 384
SPAN = 640
CHUNKS = PLANE // SPAN
SHARES = 16
SHARE = NZ * PLANE // SHARES

filter_center = 5.5
filter_radius = 4.5


def filter_kernel(mixed_ref, rim_ref, out_ref, one, two, rim_term, pot):
    x = lax.rem(lax.broadcasted_iota(jnp.int32, (NZ, SPAN), 1), NX)
    row, col = (lax.broadcasted_iota(jnp.int32, (2 * NZ, 2 * NZ), k) for k in range(2))
    apart = jnp.where((row >= NZ) == (col >= NZ), jnp.abs(row - col), 3)
    weight = jnp.where(apart == 0, -90.0, jnp.where(apart == 1, 16.0, jnp.where(apart == 2, -1.0, 0.0)))
    z_matrix = weight.astype(jnp.bfloat16)
    first, last = x == 0, x == NX - 1
    first_two, last_two = x <= 1, x >= NX - 2

    def wrap(ref, orb):
        ref[orb, :, 0:PAD] = ref[orb, :, PLANE : PLANE + PAD]
        ref[orb, :, PAD + PLANE : 2 * PAD + PLANE] = ref[orb, :, PAD : 2 * PAD]

    pot[...] = jnp.concatenate([mixed_ref[s, 2] for s in range(4)], axis=0).astype(jnp.float32)
    for orb in range(2):
        planes = [mixed_ref[s, orb] for s in range(4)]
        one[orb, :, PAD : PAD + PLANE] = jnp.concatenate(planes, axis=0).astype(jnp.float32)
        wrap(one, orb)
        rim = rim_ref[orb].astype(jnp.float32)
        low_far, low, high, high_far = (rim[k : k + 1] for k in range(4))
        rim_term[orb] = jnp.concatenate(
            [16.0 * low - low_far, -low, jnp.zeros((4, PLANE), jnp.float32), -high, 16.0 * high - high_far],
            axis=0,
        )

    def z_parts(ref, at):
        both = jnp.concatenate([ref[orb, :, pl.ds(at + PAD, SPAN)] for orb in range(2)], axis=0)
        return jnp.dot(z_matrix, both.astype(jnp.bfloat16), preferred_element_type=jnp.float32)

    def apply_ham(ref, orb, at, z_part):
        window = ref[orb, :, pl.ds(at, SPAN + 2 * PAD)]
        width = SPAN + 2 * PAD

        def cells(shift):
            return pltpu.roll(window, (-shift) % width, 1)[:, PAD : PAD + SPAN]

        middle = window[:, PAD : PAD + SPAN]
        near = jnp.where(first, cells(NX - 1), cells(-1)) + jnp.where(last, cells(1 - NX), cells(1))
        near = near + (cells(NX) + cells(-NX))
        far = jnp.where(first_two, cells(NX - 2), cells(-2)) + jnp.where(
            last_two, cells(2 - NX), cells(2)
        )
        far = far + (cells(2 * NX) + cells(-2 * NX))
        total = (16.0 * near - far) + z_part[NZ * orb : NZ * orb + NZ]
        total = total + rim_term[orb, :, pl.ds(at, SPAN)]
        return total * (-0.5 / 12.0) + pot[:, pl.ds(at, SPAN)] * middle, middle

    current, earlier = one, two
    for step in range(DEGREE):

        def body(chunk, carry, step=step, current=current, earlier=earlier):
            at = chunk * SPAN
            z_part = z_parts(current, at)
            for orb in range(2):
                with_h, middle = apply_ham(current, orb, at, z_part)
                following = (with_h - filter_center * middle) * (1.0 / filter_radius)
                place = (orb, slice(None), pl.ds(at + PAD, SPAN))
                if step > 0:
                    following = 2.0 * following - earlier[place]
                earlier[place] = following.astype(jnp.bfloat16).astype(jnp.float32)
            return carry

        for chunk in range(CHUNKS):
            body(chunk, 0)
        for orb in range(2):
            wrap(earlier, orb)
        current, earlier = earlier, current

    def last_body(chunk, carry):
        at = chunk * SPAN
        z_part = z_parts(current, at)
        for orb in range(2):
            with_h, middle = apply_ham(current, orb, at, z_part)
            out_ref[orb, :, pl.ds(at, SPAN)] = middle.astype(jnp.bfloat16)
            out_ref[2 + orb, :, pl.ds(at, SPAN)] = with_h.astype(jnp.bfloat16)
        return carry

    for chunk in range(CHUNKS):
        last_body(chunk, 0)


def filtered_and_applied(mixed, rim):
    whole = pl.BlockSpec(memory_space=pltpu.VMEM)
    return pl.pallas_call(
        filter_kernel,
        in_specs=[whole, whole],
        out_specs=whole,
        out_shape=jax.ShapeDtypeStruct((4, NZ, PLANE), jnp.bfloat16),
        scratch_shapes=[
            pltpu.VMEM((2, NZ, PLANE + 2 * PAD), jnp.float32),
            pltpu.VMEM((2, NZ, PLANE + 2 * PAD), jnp.float32),
            pltpu.VMEM((2, NZ, PLANE), jnp.float32),
            pltpu.VMEM((NZ, PLANE), jnp.float32),
        ],
        compiler_params=pltpu.CompilerParams(vmem_limit_bytes=24 * 1024 * 1024),
        name="chebyshev_filter",
    )(mixed, rim)


def swapped(values):
    return pltpu.roll(values, 64, 1)


def product_kernel(core_ref, own_ref, other_ref, cols_ref, out_ref, blocks):
    core = core_ref[0]
    cols = jnp.concatenate(
        [cols_ref[y, 16 * zh : 16 * zh + 16, :] for zh in range(4) for y in range(4)], axis=0
    )
    left = lax.broadcasted_iota(jnp.int32, (64, 128), 1) < 64
    for rows_ref, place in ((own_ref, core), (other_ref, 1 - core)):
        block = lax.dot_general(
            rows_ref[...], cols, (((1,), (1,)), ((), ())), preferred_element_type=jnp.float32
        )
        for pair in range(2):
            low = block[:64, 128 * pair : 128 * pair + 128]
            high = block[64:, 128 * pair : 128 * pair + 128]
            blocks[place, 2 * pair] = jnp.where(left, low, swapped(high))
            blocks[place, 2 * pair + 1] = jnp.where(left, swapped(low), high)
    for z in range(16):
        for xl in range(2):
            for zh in range(4):
                for c in range(2):
                    out_ref[(z * 2 + xl) * 4 + zh, 2 * c : 2 * c + 2, :] = blocks[
                        c, zh, xl * 32 + z * 2 : xl * 32 + z * 2 + 2, :
                    ]


def block_product(core, own, other, cols):
    whole = pl.BlockSpec(memory_space=pltpu.VMEM)
    return pl.pallas_call(
        product_kernel,
        in_specs=[pl.BlockSpec(memory_space=pltpu.SMEM), whole, whole, whole],
        out_specs=whole,
        out_shape=jax.ShapeDtypeStruct((128, 4, 128), jnp.float32),
        scratch_shapes=[pltpu.VMEM((2, 4, 64, 128), jnp.float32)],
        compiler_params=pltpu.CompilerParams(vmem_limit_bytes=24 * 1024 * 1024),
        name="block_product",
    )(core, own, other, cols)


def finish_kernel(parts_ref, correlation_ref, projected_ref):
    left = lax.broadcasted_iota(jnp.int32, (4, 128), 1) < 64
    pieces = []
    for pair in range(4):
        one, two = parts_ref[2 * pair], parts_ref[2 * pair + 1]
        for k in range(1, 16):
            one = one + parts_ref[8 * k + 2 * pair]
            two = two + parts_ref[8 * k + 2 * pair + 1]
        low = jnp.where(left, one, swapped(two))
        high = jnp.where(left, swapped(one), two)
        pieces.append(jnp.concatenate([low, high], axis=0))
    given = jnp.concatenate(pieces, axis=1) * (1.0 / (NZ * PLANE))
    at = lax.broadcasted_iota(jnp.int32, (1, 512), 1)

    def field(shift, count):
        return lax.shift_right_logical(at, shift) & (count - 1)

    group = field(3, 2) * 4 + field(1, 4)
    source = group * 64 + field(4, 4) * 16 + field(6, 4) * 4 + field(8, 2) * 2 + field(0, 2)
    hot = jnp.where(lax.broadcasted_iota(jnp.int32, (512, 512), 0) == source, 1.0, 0.0)
    top = given.astype(jnp.bfloat16)
    rest = given - top.astype(jnp.float32)
    middle = rest.astype(jnp.bfloat16)
    last = (rest - middle.astype(jnp.float32)).astype(jnp.bfloat16)
    split = jnp.concatenate(
        [top.astype(jnp.float32), middle.astype(jnp.float32), last.astype(jnp.float32)], axis=0
    )
    placed = jnp.dot(
        split.astype(jnp.bfloat16), hot.astype(jnp.bfloat16), preferred_element_type=jnp.float32
    )
    placed = (placed[16:] + placed[8:16]) + placed[:8]
    correlation_ref[...] = placed[:, :256]
    projected_ref[...] = placed[:, 256:]


def finish(parts):
    shape = jax.ShapeDtypeStruct((8, 256), jnp.float32)
    whole = pl.BlockSpec(memory_space=pltpu.VMEM)
    return pl.pallas_call(
        finish_kernel,
        in_specs=[whole],
        out_specs=[whole, whole],
        out_shape=[shape, shape],
        compiler_params=pltpu.CompilerParams(vmem_limit_bytes=8 * 1024 * 1024),
        name="finish",
    )(parts)


def pieces_kernel(orbitals_ref, potential_ref, out_ref, sems):
    copies = [pltpu.make_async_copy(orbitals_ref, out_ref.at[:, 0:2], sems.at[0])]
    for k in range(4):
        copies.append(pltpu.make_async_copy(potential_ref, out_ref.at[k, 2], sems.at[1 + k]))
    for copy in copies:
        copy.start()
    for copy in copies:
        copy.wait()


def pieces_of(orbitals, potential):
    anywhere = pl.BlockSpec(memory_space=pl.ANY)
    return pl.pallas_call(
        pieces_kernel,
        in_specs=[anywhere, anywhere],
        out_specs=pl.BlockSpec(memory_space=pltpu.VMEM),
        out_shape=jax.ShapeDtypeStruct((4, 3, 2, PLANE), jnp.bfloat16),
        scratch_shapes=[pltpu.SemaphoreType.DMA((5,))],
        compiler_params=pltpu.CompilerParams(vmem_limit_bytes=56 * 1024 * 1024),
        name="pieces",
    )(orbitals, potential)


def per_device(orbitals, boundary, potential):
    own = lax.axis_index("xh") * 2 + lax.axis_index("c")
    pieces = pieces_of(orbitals.reshape(4, 2, 2, PLANE), potential)
    mixed = lax.all_to_all(pieces, ("xh", "c"), split_axis=0, concat_axis=0, tiled=True)
    rim = lax.dynamic_index_in_dim(boundary.reshape(4, 2, 4, PLANE), own, 0, keepdims=False)
    fields = filtered_and_applied(mixed, rim)
    shares = fields.reshape(4, SHARES, SHARE).transpose(1, 0, 2)
    shares = lax.all_to_all(shares, "z", split_axis=0, concat_axis=0, tiled=True)
    cols = shares.reshape(4 * SHARES, SHARE)
    cols = lax.all_to_all(
        jnp.broadcast_to(cols[None], (4, 4 * SHARES, SHARE)), "y", split_axis=0, concat_axis=0, tiled=True
    )
    rows = shares[:, :2].reshape(2 * SHARES, SHARE)
    rows = lax.all_gather(rows, ("xh", "xl"), axis=0, tiled=True)
    other = lax.ppermute(rows, "c", [(0, 1), (1, 0)])
    core = lax.axis_index("c").astype(jnp.int32).reshape(1)
    partial = block_product(core, rows, other, cols)
    parts = lax.all_to_all(partial, ("z", "xl", "xh", "c"), split_axis=0, concat_axis=0, tiled=True)
    return tuple(finish(parts))


def solution(mesh):
    split = Mesh(mesh.devices.reshape(16, 4, 2, 2, 2), ("z", "y", "xl", "xh", "c"))
    band, domain = ("z", "y", "xl"), ("xh", "c")
    return jax.shard_map(
        per_device,
        mesh=split,
        in_specs=(P(band, domain, None), P(band, None, None), P(domain, None)),
        out_specs=(P(band, domain), P(band, domain)),
        check_vma=False,
    )
```

```python
import jax
import jax.numpy as jnp
from jax import lax
from jax.experimental import pallas as pl
from jax.experimental.pallas import tpu as pltpu
from jax.sharding import Mesh, PartitionSpec as P

NX = 160
NY = 32
NZ = 8
PLANE = NX * NY
DEGREE = 4
PAD = 384
SPAN = 640
CHUNKS = PLANE // SPAN
SHARES = 16
SHARE = NZ * PLANE // SHARES

filter_center = 5.5
filter_radius = 4.5


def filter_kernel(mixed_ref, rim_ref, out_ref, one, two, rim_term, pot):
    x = lax.rem(lax.broadcasted_iota(jnp.int32, (NZ, SPAN), 1), NX)
    row, col = (lax.broadcasted_iota(jnp.int32, (2 * NZ, 2 * NZ), k) for k in range(2))
    apart = jnp.where((row >= NZ) == (col >= NZ), jnp.abs(row - col), 3)
    weight = jnp.where(apart == 0, -90.0, jnp.where(apart == 1, 16.0, jnp.where(apart == 2, -1.0, 0.0)))
    z_matrix = weight.astype(jnp.bfloat16)
    first, last = x == 0, x == NX - 1
    first_two, last_two = x <= 1, x >= NX - 2

    def wrap(ref, orb):
        ref[orb, :, 0:PAD] = ref[orb, :, PLANE : PLANE + PAD]
        ref[orb, :, PAD + PLANE : 2 * PAD + PLANE] = ref[orb, :, PAD : 2 * PAD]

    pot[...] = jnp.concatenate([mixed_ref[s, 2] for s in range(4)], axis=0).astype(jnp.float32)
    for orb in range(2):
        planes = [mixed_ref[s, orb] for s in range(4)]
        one[orb, :, PAD : PAD + PLANE] = jnp.concatenate(planes, axis=0).astype(jnp.float32)
        wrap(one, orb)
        rim = rim_ref[orb].astype(jnp.float32)
        low_far, low, high, high_far = (rim[k : k + 1] for k in range(4))
        rim_term[orb] = jnp.concatenate(
            [16.0 * low - low_far, -low, jnp.zeros((4, PLANE), jnp.float32), -high, 16.0 * high - high_far],
            axis=0,
        )

    def z_parts(ref, at):
        both = jnp.concatenate([ref[orb, :, pl.ds(at + PAD, SPAN)] for orb in range(2)], axis=0)
        return jnp.dot(z_matrix, both.astype(jnp.bfloat16), preferred_element_type=jnp.float32)

    def apply_ham(ref, orb, at, z_part):
        window = ref[orb, :, pl.ds(at, SPAN + 2 * PAD)]
        width = SPAN + 2 * PAD

        def cells(shift):
            return pltpu.roll(window, (-shift) % width, 1)[:, PAD : PAD + SPAN]

        middle = window[:, PAD : PAD + SPAN]
        near = jnp.where(first, cells(NX - 1), cells(-1)) + jnp.where(last, cells(1 - NX), cells(1))
        near = near + (cells(NX) + cells(-NX))
        far = jnp.where(first_two, cells(NX - 2), cells(-2)) + jnp.where(
            last_two, cells(2 - NX), cells(2)
        )
        far = far + (cells(2 * NX) + cells(-2 * NX))
        total = (16.0 * near - far) + z_part[NZ * orb : NZ * orb + NZ]
        total = total + rim_term[orb, :, pl.ds(at, SPAN)]
        return total * (-0.5 / 12.0) + pot[:, pl.ds(at, SPAN)] * middle, middle

    current, earlier = one, two
    for step in range(DEGREE):

        def body(chunk, carry, step=step, current=current, earlier=earlier):
            at = chunk * SPAN
            z_part = z_parts(current, at)
            for orb in range(2):
                with_h, middle = apply_ham(current, orb, at, z_part)
                following = (with_h - filter_center * middle) * (1.0 / filter_radius)
                place = (orb, slice(None), pl.ds(at + PAD, SPAN))
                if step > 0:
                    following = 2.0 * following - earlier[place]
                earlier[place] = following.astype(jnp.bfloat16).astype(jnp.float32)
            return carry

        for chunk in range(CHUNKS):
            body(chunk, 0)
        for orb in range(2):
            wrap(earlier, orb)
        current, earlier = earlier, current

    def last_body(chunk, carry):
        at = chunk * SPAN
        z_part = z_parts(current, at)
        for orb in range(2):
            with_h, middle = apply_ham(current, orb, at, z_part)
            out_ref[orb, :, pl.ds(at, SPAN)] = middle.astype(jnp.bfloat16)
            out_ref[2 + orb, :, pl.ds(at, SPAN)] = with_h.astype(jnp.bfloat16)
        return carry

    for chunk in range(CHUNKS):
        last_body(chunk, 0)


def filtered_and_applied(mixed, rim):
    whole = pl.BlockSpec(memory_space=pltpu.VMEM)
    return pl.pallas_call(
        filter_kernel,
        in_specs=[whole, whole],
        out_specs=whole,
        out_shape=jax.ShapeDtypeStruct((4, NZ, PLANE), jnp.bfloat16),
        scratch_shapes=[
            pltpu.VMEM((2, NZ, PLANE + 2 * PAD), jnp.float32),
            pltpu.VMEM((2, NZ, PLANE + 2 * PAD), jnp.float32),
            pltpu.VMEM((2, NZ, PLANE), jnp.float32),
            pltpu.VMEM((NZ, PLANE), jnp.float32),
        ],
        compiler_params=pltpu.CompilerParams(vmem_limit_bytes=24 * 1024 * 1024),
        name="chebyshev_filter",
    )(mixed, rim)


def swapped(values):
    return pltpu.roll(values, 64, 1)


def product_kernel(core_ref, own_ref, other_ref, cols_ref, out_ref, blocks):
    core = core_ref[0]
    cols = jnp.concatenate(
        [cols_ref[y, 16 * zh : 16 * zh + 16, :] for zh in range(4) for y in range(4)], axis=0
    )
    left = lax.broadcasted_iota(jnp.int32, (64, 128), 1) < 64
    for rows_ref, place in ((own_ref, core), (other_ref, 1 - core)):
        block = lax.dot_general(
            rows_ref[...], cols, (((1,), (1,)), ((), ())), preferred_element_type=jnp.float32
        )
        for pair in range(2):
            low = block[:64, 128 * pair : 128 * pair + 128]
            high = block[64:, 128 * pair : 128 * pair + 128]
            blocks[place, 2 * pair] = jnp.where(left, low, swapped(high))
            blocks[place, 2 * pair + 1] = jnp.where(left, swapped(low), high)
    for z in range(16):
        for xl in range(2):
            for zh in range(4):
                for c in range(2):
                    out_ref[(z * 2 + xl) * 4 + zh, 2 * c : 2 * c + 2, :] = blocks[
                        c, zh, xl * 32 + z * 2 : xl * 32 + z * 2 + 2, :
                    ]


def block_product(core, own, other, cols):
    whole = pl.BlockSpec(memory_space=pltpu.VMEM)
    return pl.pallas_call(
        product_kernel,
        in_specs=[pl.BlockSpec(memory_space=pltpu.SMEM), whole, whole, whole],
        out_specs=whole,
        out_shape=jax.ShapeDtypeStruct((128, 4, 128), jnp.float32),
        scratch_shapes=[pltpu.VMEM((2, 4, 64, 128), jnp.float32)],
        compiler_params=pltpu.CompilerParams(vmem_limit_bytes=24 * 1024 * 1024),
        name="block_product",
    )(core, own, other, cols)


def places_kernel(hot_ref):
    at = lax.broadcasted_iota(jnp.int32, (1, 512), 1)

    def field(shift, count):
        return lax.shift_right_logical(at, shift) & (count - 1)

    group = field(3, 2) * 4 + field(1, 4)
    source = group * 64 + field(4, 4) * 16 + field(6, 4) * 4 + field(8, 2) * 2 + field(0, 2)
    hot = jnp.where(lax.broadcasted_iota(jnp.int32, (512, 512), 0) == source, 1.0, 0.0)
    hot_ref[...] = hot.astype(jnp.bfloat16)


def places():
    return pl.pallas_call(
        places_kernel,
        out_specs=pl.BlockSpec(memory_space=pltpu.VMEM),
        out_shape=jax.ShapeDtypeStruct((512, 512), jnp.bfloat16),
        compiler_params=pltpu.CompilerParams(vmem_limit_bytes=8 * 1024 * 1024),
        cost_estimate=pl.CostEstimate(flops=1000000, bytes_accessed=524288, transcendentals=0),
        name="places",
    )()


def finish_kernel(parts_ref, hot_ref, correlation_ref, projected_ref):
    left = lax.broadcasted_iota(jnp.int32, (4, 128), 1) < 64
    pieces = []
    for pair in range(4):
        one, two = parts_ref[2 * pair], parts_ref[2 * pair + 1]
        for k in range(1, 16):
            one = one + parts_ref[8 * k + 2 * pair]
            two = two + parts_ref[8 * k + 2 * pair + 1]
        low = jnp.where(left, one, swapped(two))
        high = jnp.where(left, swapped(one), two)
        pieces.append(jnp.concatenate([low, high], axis=0))
    given = jnp.concatenate(pieces, axis=1) * (1.0 / (NZ * PLANE))
    top = given.astype(jnp.bfloat16)
    rest = given - top.astype(jnp.float32)
    middle = rest.astype(jnp.bfloat16)
    last = (rest - middle.astype(jnp.float32)).astype(jnp.bfloat16)
    split = jnp.concatenate(
        [top.astype(jnp.float32), middle.astype(jnp.float32), last.astype(jnp.float32)], axis=0
    )
    placed = jnp.dot(
        split.astype(jnp.bfloat16), hot_ref[...], preferred_element_type=jnp.float32
    )
    placed = (placed[16:] + placed[8:16]) + placed[:8]
    correlation_ref[...] = placed[:, :256]
    projected_ref[...] = placed[:, 256:]


def finish(parts, hot):
    shape = jax.ShapeDtypeStruct((8, 256), jnp.float32)
    whole = pl.BlockSpec(memory_space=pltpu.VMEM)
    return pl.pallas_call(
        finish_kernel,
        in_specs=[whole, whole],
        out_specs=[whole, whole],
        out_shape=[shape, shape],
        compiler_params=pltpu.CompilerParams(vmem_limit_bytes=8 * 1024 * 1024),
        name="finish",
    )(parts, hot)


def pieces_kernel(orbitals_ref, potential_ref, out_ref, sems):
    copies = [pltpu.make_async_copy(orbitals_ref, out_ref.at[:, 0:2], sems.at[0])]
    for k in range(4):
        copies.append(pltpu.make_async_copy(potential_ref, out_ref.at[k, 2], sems.at[1 + k]))
    for copy in copies:
        copy.start()
    for copy in copies:
        copy.wait()


def pieces_of(orbitals, potential):
    anywhere = pl.BlockSpec(memory_space=pl.ANY)
    return pl.pallas_call(
        pieces_kernel,
        in_specs=[anywhere, anywhere],
        out_specs=pl.BlockSpec(memory_space=pltpu.VMEM),
        out_shape=jax.ShapeDtypeStruct((4, 3, 2, PLANE), jnp.bfloat16),
        scratch_shapes=[pltpu.SemaphoreType.DMA((5,))],
        compiler_params=pltpu.CompilerParams(vmem_limit_bytes=56 * 1024 * 1024),
        name="pieces",
    )(orbitals, potential)


def spread_kernel(values_ref, out_ref, sems):
    copies = [pltpu.make_async_copy(values_ref, out_ref.at[k], sems.at[k]) for k in range(4)]
    for copy in copies:
        copy.start()
    for copy in copies:
        copy.wait()


def spread(values):
    return pl.pallas_call(
        spread_kernel,
        in_specs=[pl.BlockSpec(memory_space=pltpu.VMEM)],
        out_specs=pl.BlockSpec(memory_space=pl.ANY),
        out_shape=jax.ShapeDtypeStruct((4,) + values.shape, values.dtype),
        scratch_shapes=[pltpu.SemaphoreType.DMA((4,))],
        compiler_params=pltpu.CompilerParams(vmem_limit_bytes=4 * 1024 * 1024),
        name="spread",
    )(values)


def per_device(orbitals, boundary, potential):
    own = lax.axis_index("xh") * 2 + lax.axis_index("c")
    pieces = pieces_of(orbitals.reshape(4, 2, 2, PLANE), potential)
    mixed = lax.all_to_all(pieces, ("xh", "c"), split_axis=0, concat_axis=0, tiled=True)
    hot = places()
    rim = lax.dynamic_index_in_dim(boundary.reshape(4, 2, 4, PLANE), own, 0, keepdims=False)
    fields = filtered_and_applied(mixed, rim)
    shares = fields.reshape(4, SHARES, SHARE).transpose(1, 0, 2)
    shares = lax.all_to_all(shares, "z", split_axis=0, concat_axis=0, tiled=True)
    cols = shares.reshape(4 * SHARES, SHARE)
    cols = lax.all_to_all(spread(cols), "y", split_axis=0, concat_axis=0, tiled=True)
    rows = shares[:, :2].reshape(2 * SHARES, SHARE)
    rows = lax.all_gather(rows, ("xh", "xl"), axis=0, tiled=True)
    other = lax.ppermute(rows, "c", [(0, 1), (1, 0)])
    core = lax.axis_index("c").astype(jnp.int32).reshape(1)
    partial = block_product(core, rows, other, cols)
    parts = lax.all_to_all(partial, ("z", "xl", "xh", "c"), split_axis=0, concat_axis=0, tiled=True)
    return tuple(finish(parts, hot))


def solution(mesh):
    split = Mesh(mesh.devices.reshape(16, 4, 2, 2, 2), ("z", "y", "xl", "xh", "c"))
    band, domain = ("z", "y", "xl"), ("xh", "c")
    return jax.shard_map(
        per_device,
        mesh=split,
        in_specs=(P(band, domain, None), P(band, None, None), P(domain, None)),
        out_specs=(P(band, domain), P(band, domain)),
        check_vma=False,
    )
```

```python
import jax
import jax.numpy as jnp
from jax import lax
from jax.experimental import pallas as pl
from jax.experimental.pallas import tpu as pltpu
from jax.sharding import Mesh, PartitionSpec as P

NX = 160
NY = 32
NZ = 8
PLANE = NX * NY
DEGREE = 4
PAD = 384
SPAN = 640
CHUNKS = PLANE // SPAN
SHARES = 16
SHARE = NZ * PLANE // SHARES

filter_center = 5.5
filter_radius = 4.5


def filter_kernel(mixed_ref, rim_ref, out_ref, one, two, rim_term, pot):
    x = lax.rem(lax.broadcasted_iota(jnp.int32, (NZ, SPAN), 1), NX)
    row, col = (lax.broadcasted_iota(jnp.int32, (2 * NZ, 2 * NZ), k) for k in range(2))
    apart = jnp.where((row >= NZ) == (col >= NZ), jnp.abs(row - col), 3)
    weight = jnp.where(apart == 0, -90.0, jnp.where(apart == 1, 16.0, jnp.where(apart == 2, -1.0, 0.0)))
    z_matrix = weight.astype(jnp.bfloat16)
    first, last = x == 0, x == NX - 1
    first_two, last_two = x <= 1, x >= NX - 2

    def wrap(ref, orb):
        ref[orb, :, 0:PAD] = ref[orb, :, PLANE : PLANE + PAD]
        ref[orb, :, PAD + PLANE : 2 * PAD + PLANE] = ref[orb, :, PAD : 2 * PAD]

    pot[...] = jnp.concatenate([mixed_ref[s, 2] for s in range(4)], axis=0).astype(jnp.float32)
    for orb in range(2):
        planes = [mixed_ref[s, orb] for s in range(4)]
        one[orb, :, PAD : PAD + PLANE] = jnp.concatenate(planes, axis=0).astype(jnp.float32)
        wrap(one, orb)
        rim = rim_ref[orb].astype(jnp.float32)
        low_far, low, high, high_far = (rim[k : k + 1] for k in range(4))
        rim_term[orb] = jnp.concatenate(
            [16.0 * low - low_far, -low, jnp.zeros((4, PLANE), jnp.float32), -high, 16.0 * high - high_far],
            axis=0,
        )

    def z_parts(ref, at):
        both = jnp.concatenate([ref[orb, :, pl.ds(at + PAD, SPAN)] for orb in range(2)], axis=0)
        return jnp.dot(z_matrix, both.astype(jnp.bfloat16), preferred_element_type=jnp.float32)

    def apply_ham(ref, orb, at, z_part):
        window = ref[orb, :, pl.ds(at, SPAN + 2 * PAD)]
        width = SPAN + 2 * PAD

        def cells(shift):
            return pltpu.roll(window, (-shift) % width, 1)[:, PAD : PAD + SPAN]

        middle = window[:, PAD : PAD + SPAN]
        near = jnp.where(first, cells(NX - 1), cells(-1)) + jnp.where(last, cells(1 - NX), cells(1))
        near = near + (cells(NX) + cells(-NX))
        far = jnp.where(first_two, cells(NX - 2), cells(-2)) + jnp.where(
            last_two, cells(2 - NX), cells(2)
        )
        far = far + (cells(2 * NX) + cells(-2 * NX))
        total = (16.0 * near - far) + z_part[NZ * orb : NZ * orb + NZ]
        total = total + rim_term[orb, :, pl.ds(at, SPAN)]
        return total * (-0.5 / 12.0) + pot[:, pl.ds(at, SPAN)] * middle, middle

    current, earlier = one, two
    for step in range(DEGREE):

        def body(chunk, carry, step=step, current=current, earlier=earlier):
            at = chunk * SPAN
            z_part = z_parts(current, at)
            for orb in range(2):
                with_h, middle = apply_ham(current, orb, at, z_part)
                following = (with_h - filter_center * middle) * (1.0 / filter_radius)
                place = (orb, slice(None), pl.ds(at + PAD, SPAN))
                if step > 0:
                    following = 2.0 * following - earlier[place]
                earlier[place] = following.astype(jnp.bfloat16).astype(jnp.float32)
            return carry

        for chunk in range(CHUNKS):
            body(chunk, 0)
        for orb in range(2):
            wrap(earlier, orb)
        current, earlier = earlier, current

    def last_body(chunk, carry):
        at = chunk * SPAN
        z_part = z_parts(current, at)
        for orb in range(2):
            with_h, middle = apply_ham(current, orb, at, z_part)
            out_ref[orb, :, pl.ds(at, SPAN)] = middle.astype(jnp.bfloat16)
            out_ref[2 + orb, :, pl.ds(at, SPAN)] = with_h.astype(jnp.bfloat16)
        return carry

    for chunk in range(CHUNKS):
        last_body(chunk, 0)


def filtered_and_applied(mixed, rim):
    whole = pl.BlockSpec(memory_space=pltpu.VMEM)
    return pl.pallas_call(
        filter_kernel,
        in_specs=[whole, whole],
        out_specs=whole,
        out_shape=jax.ShapeDtypeStruct((4, NZ, PLANE), jnp.bfloat16),
        scratch_shapes=[
            pltpu.VMEM((2, NZ, PLANE + 2 * PAD), jnp.float32),
            pltpu.VMEM((2, NZ, PLANE + 2 * PAD), jnp.float32),
            pltpu.VMEM((2, NZ, PLANE), jnp.float32),
            pltpu.VMEM((NZ, PLANE), jnp.float32),
        ],
        compiler_params=pltpu.CompilerParams(vmem_limit_bytes=24 * 1024 * 1024),
        name="chebyshev_filter",
    )(mixed, rim)


def swapped(values):
    return pltpu.roll(values, 64, 1)


def half_product(rows_ref, cols_ref):
    cols = jnp.concatenate(
        [cols_ref[y, 16 * zh : 16 * zh + 16, :] for zh in range(4) for y in range(4)], axis=0
    )
    left = lax.broadcasted_iota(jnp.int32, (64, 128), 1) < 64
    block = lax.dot_general(
        rows_ref[...], cols, (((1,), (1,)), ((), ())), preferred_element_type=jnp.float32
    )
    pieces = []
    for pair in range(2):
        low = block[:64, 128 * pair : 128 * pair + 128]
        high = block[64:, 128 * pair : 128 * pair + 128]
        pieces += [jnp.where(left, low, swapped(high)), jnp.where(left, swapped(low), high)]
    return pieces


def own_kernel(own_ref, cols_ref, out_ref):
    for zh, piece in enumerate(half_product(own_ref, cols_ref)):
        out_ref[zh] = piece


def join_kernel(core_ref, done_ref, other_ref, cols_ref, out_ref, blocks):
    core = core_ref[0]
    for zh, piece in enumerate(half_product(other_ref, cols_ref)):
        blocks[1 - core, zh] = piece
        blocks[core, zh] = done_ref[zh]
    for z in range(16):
        for xl in range(2):
            for zh in range(4):
                for c in range(2):
                    out_ref[(z * 2 + xl) * 4 + zh, 2 * c : 2 * c + 2, :] = blocks[
                        c, zh, xl * 32 + z * 2 : xl * 32 + z * 2 + 2, :
                    ]


def own_product(own, cols):
    whole = pl.BlockSpec(memory_space=pltpu.VMEM)
    return pl.pallas_call(
        own_kernel,
        in_specs=[whole, whole],
        out_specs=whole,
        out_shape=jax.ShapeDtypeStruct((4, 64, 128), jnp.float32),
        compiler_params=pltpu.CompilerParams(vmem_limit_bytes=24 * 1024 * 1024),
        cost_estimate=pl.CostEstimate(flops=2 * 128 * 256 * SHARE, bytes_accessed=2000000, transcendentals=0),
        name="own_product",
    )(own, cols)


def joined(core, done, other, cols):
    whole = pl.BlockSpec(memory_space=pltpu.VMEM)
    return pl.pallas_call(
        join_kernel,
        in_specs=[pl.BlockSpec(memory_space=pltpu.SMEM), whole, whole, whole],
        out_specs=whole,
        out_shape=jax.ShapeDtypeStruct((128, 4, 128), jnp.float32),
        scratch_shapes=[pltpu.VMEM((2, 4, 64, 128), jnp.float32)],
        compiler_params=pltpu.CompilerParams(vmem_limit_bytes=24 * 1024 * 1024),
        name="joined",
    )(core, done, other, cols)


def finish_kernel(parts_ref, correlation_ref, projected_ref):
    left = lax.broadcasted_iota(jnp.int32, (4, 128), 1) < 64
    pieces = []
    for pair in range(4):
        one, two = parts_ref[2 * pair], parts_ref[2 * pair + 1]
        for k in range(1, 16):
            one = one + parts_ref[8 * k + 2 * pair]
            two = two + parts_ref[8 * k + 2 * pair + 1]
        low = jnp.where(left, one, swapped(two))
        high = jnp.where(left, swapped(one), two)
        pieces.append(jnp.concatenate([low, high], axis=0))
    given = jnp.concatenate(pieces, axis=1) * (1.0 / (NZ * PLANE))
    at = lax.broadcasted_iota(jnp.int32, (1, 512), 1)

    def field(shift, count):
        return lax.shift_right_logical(at, shift) & (count - 1)

    group = field(3, 2) * 4 + field(1, 4)
    source = group * 64 + field(4, 4) * 16 + field(6, 4) * 4 + field(8, 2) * 2 + field(0, 2)
    hot = jnp.where(lax.broadcasted_iota(jnp.int32, (512, 512), 0) == source, 1.0, 0.0)
    top = given.astype(jnp.bfloat16)
    rest = given - top.astype(jnp.float32)
    middle = rest.astype(jnp.bfloat16)
    last = (rest - middle.astype(jnp.float32)).astype(jnp.bfloat16)
    split = jnp.concatenate(
        [top.astype(jnp.float32), middle.astype(jnp.float32), last.astype(jnp.float32)], axis=0
    )
    placed = jnp.dot(
        split.astype(jnp.bfloat16), hot.astype(jnp.bfloat16), preferred_element_type=jnp.float32
    )
    placed = (placed[16:] + placed[8:16]) + placed[:8]
    correlation_ref[...] = placed[:, :256]
    projected_ref[...] = placed[:, 256:]


def finish(parts):
    shape = jax.ShapeDtypeStruct((8, 256), jnp.float32)
    whole = pl.BlockSpec(memory_space=pltpu.VMEM)
    return pl.pallas_call(
        finish_kernel,
        in_specs=[whole],
        out_specs=[whole, whole],
        out_shape=[shape, shape],
        compiler_params=pltpu.CompilerParams(vmem_limit_bytes=8 * 1024 * 1024),
        name="finish",
    )(parts)


def pieces_kernel(orbitals_ref, potential_ref, out_ref, sems):
    copies = [pltpu.make_async_copy(orbitals_ref, out_ref.at[:, 0:2], sems.at[0])]
    for k in range(4):
        copies.append(pltpu.make_async_copy(potential_ref, out_ref.at[k, 2], sems.at[1 + k]))
    for copy in copies:
        copy.start()
    for copy in copies:
        copy.wait()


def pieces_of(orbitals, potential):
    anywhere = pl.BlockSpec(memory_space=pl.ANY)
    return pl.pallas_call(
        pieces_kernel,
        in_specs=[anywhere, anywhere],
        out_specs=pl.BlockSpec(memory_space=pltpu.VMEM),
        out_shape=jax.ShapeDtypeStruct((4, 3, 2, PLANE), jnp.bfloat16),
        scratch_shapes=[pltpu.SemaphoreType.DMA((5,))],
        compiler_params=pltpu.CompilerParams(vmem_limit_bytes=56 * 1024 * 1024),
        name="pieces",
    )(orbitals, potential)


def per_device(orbitals, boundary, potential):
    own = lax.axis_index("xh") * 2 + lax.axis_index("c")
    pieces = pieces_of(orbitals.reshape(4, 2, 2, PLANE), potential)
    mixed = lax.all_to_all(pieces, ("xh", "c"), split_axis=0, concat_axis=0, tiled=True)
    rim = lax.dynamic_index_in_dim(boundary.reshape(4, 2, 4, PLANE), own, 0, keepdims=False)
    fields = filtered_and_applied(mixed, rim)
    shares = fields.reshape(4, SHARES, SHARE).transpose(1, 0, 2)
    shares = lax.all_to_all(shares, "z", split_axis=0, concat_axis=0, tiled=True)
    cols = shares.reshape(4 * SHARES, SHARE)
    cols = lax.all_to_all(
        jnp.broadcast_to(cols[None], (4, 4 * SHARES, SHARE)), "y", split_axis=0, concat_axis=0, tiled=True
    )
    rows = shares[:, :2].reshape(2 * SHARES, SHARE)
    rows = lax.all_gather(rows, ("xh", "xl"), axis=0, tiled=True)
    other = lax.ppermute(rows, "c", [(0, 1), (1, 0)])
    core = lax.axis_index("c").astype(jnp.int32).reshape(1)
    partial = joined(core, own_product(rows, cols), other, cols)
    parts = lax.all_to_all(partial, ("z", "xl", "xh", "c"), split_axis=0, concat_axis=0, tiled=True)
    return tuple(finish(parts))


def solution(mesh):
    split = Mesh(mesh.devices.reshape(16, 4, 2, 2, 2), ("z", "y", "xl", "xh", "c"))
    band, domain = ("z", "y", "xl"), ("xh", "c")
    return jax.shard_map(
        per_device,
        mesh=split,
        in_specs=(P(band, domain, None), P(band, None, None), P(domain, None)),
        out_specs=(P(band, domain), P(band, domain)),
        check_vma=False,
    )
```

```python
import jax
import jax.numpy as jnp
from jax import lax
from jax.experimental import pallas as pl
from jax.experimental.pallas import tpu as pltpu
from jax.sharding import Mesh, PartitionSpec as P

NX = 160
NY = 32
NZ = 8
PLANE = NX * NY
DEGREE = 4
PAD = 384
SPAN = 640
CHUNKS = PLANE // SPAN
SHARES = 16
SHARE = NZ * PLANE // SHARES

filter_center = 5.5
filter_radius = 4.5


def filter_kernel(mixed_ref, rim_ref, out_ref, one, two, rim_term, pot):
    x = lax.rem(lax.broadcasted_iota(jnp.int32, (NZ, SPAN), 1), NX)
    row, col = (lax.broadcasted_iota(jnp.int32, (2 * NZ, 2 * NZ), k) for k in range(2))
    apart = jnp.where((row >= NZ) == (col >= NZ), jnp.abs(row - col), 3)
    weight = jnp.where(apart == 0, -90.0, jnp.where(apart == 1, 16.0, jnp.where(apart == 2, -1.0, 0.0)))
    z_matrix = weight.astype(jnp.bfloat16)
    first, last = x == 0, x == NX - 1
    first_two, last_two = x <= 1, x >= NX - 2

    def wrap(ref, orb):
        ref[orb, :, 0:PAD] = ref[orb, :, PLANE : PLANE + PAD]
        ref[orb, :, PAD + PLANE : 2 * PAD + PLANE] = ref[orb, :, PAD : 2 * PAD]

    pot[...] = jnp.concatenate([mixed_ref[s, 2] for s in range(4)], axis=0).astype(jnp.float32)
    for orb in range(2):
        planes = [mixed_ref[s, orb] for s in range(4)]
        one[orb, :, PAD : PAD + PLANE] = jnp.concatenate(planes, axis=0).astype(jnp.float32)
        wrap(one, orb)
        rim = rim_ref[orb].astype(jnp.float32)
        low_far, low, high, high_far = (rim[k : k + 1] for k in range(4))
        rim_term[orb] = jnp.concatenate(
            [16.0 * low - low_far, -low, jnp.zeros((4, PLANE), jnp.float32), -high, 16.0 * high - high_far],
            axis=0,
        )

    def z_parts(ref, at):
        both = jnp.concatenate([ref[orb, :, pl.ds(at + PAD, SPAN)] for orb in range(2)], axis=0)
        return jnp.dot(z_matrix, both.astype(jnp.bfloat16), preferred_element_type=jnp.float32)

    def apply_ham(ref, orb, at, z_part):
        window = ref[orb, :, pl.ds(at, SPAN + 2 * PAD)]
        width = SPAN + 2 * PAD

        def cells(shift):
            return pltpu.roll(window, (-shift) % width, 1)[:, PAD : PAD + SPAN]

        middle = window[:, PAD : PAD + SPAN]
        near = jnp.where(first, cells(NX - 1), cells(-1)) + jnp.where(last, cells(1 - NX), cells(1))
        near = near + (cells(NX) + cells(-NX))
        far = jnp.where(first_two, cells(NX - 2), cells(-2)) + jnp.where(
            last_two, cells(2 - NX), cells(2)
        )
        far = far + (cells(2 * NX) + cells(-2 * NX))
        total = (16.0 * near - far) + z_part[NZ * orb : NZ * orb + NZ]
        total = total + rim_term[orb, :, pl.ds(at, SPAN)]
        return total * (-0.5 / 12.0) + pot[:, pl.ds(at, SPAN)] * middle, middle

    current, earlier = one, two
    for step in range(DEGREE):

        def body(chunk, carry, step=step, current=current, earlier=earlier):
            at = chunk * SPAN
            z_part = z_parts(current, at)
            for orb in range(2):
                with_h, middle = apply_ham(current, orb, at, z_part)
                following = (with_h - filter_center * middle) * (1.0 / filter_radius)
                place = (orb, slice(None), pl.ds(at + PAD, SPAN))
                if step > 0:
                    following = 2.0 * following - earlier[place]
                earlier[place] = following.astype(jnp.bfloat16).astype(jnp.float32)
            return carry

        for chunk in range(CHUNKS):
            body(chunk, 0)
        for orb in range(2):
            wrap(earlier, orb)
        current, earlier = earlier, current

    def last_body(chunk, carry):
        at = chunk * SPAN
        z_part = z_parts(current, at)
        for orb in range(2):
            with_h, middle = apply_ham(current, orb, at, z_part)
            out_ref[orb, :, pl.ds(at, SPAN)] = middle.astype(jnp.bfloat16)
            out_ref[2 + orb, :, pl.ds(at, SPAN)] = with_h.astype(jnp.bfloat16)
        return carry

    for chunk in range(CHUNKS):
        last_body(chunk, 0)


def filtered_and_applied(mixed, rim):
    whole = pl.BlockSpec(memory_space=pltpu.VMEM)
    return pl.pallas_call(
        filter_kernel,
        in_specs=[whole, whole],
        out_specs=whole,
        out_shape=jax.ShapeDtypeStruct((4, NZ, PLANE), jnp.bfloat16),
        scratch_shapes=[
            pltpu.VMEM((2, NZ, PLANE + 2 * PAD), jnp.float32),
            pltpu.VMEM((2, NZ, PLANE + 2 * PAD), jnp.float32),
            pltpu.VMEM((2, NZ, PLANE), jnp.float32),
            pltpu.VMEM((NZ, PLANE), jnp.float32),
        ],
        compiler_params=pltpu.CompilerParams(vmem_limit_bytes=24 * 1024 * 1024),
        name="chebyshev_filter",
    )(mixed, rim)


def swapped(values):
    return pltpu.roll(values, 64, 1)


def half_product(rows_ref, cols_ref):
    cols = jnp.concatenate(
        [cols_ref[y, 16 * zh : 16 * zh + 16, :] for zh in range(4) for y in range(4)], axis=0
    )
    left = lax.broadcasted_iota(jnp.int32, (64, 128), 1) < 64
    block = lax.dot_general(
        rows_ref[...], cols, (((1,), (1,)), ((), ())), preferred_element_type=jnp.float32
    )
    pieces = []
    for pair in range(2):
        low = block[:64, 128 * pair : 128 * pair + 128]
        high = block[64:, 128 * pair : 128 * pair + 128]
        pieces += [jnp.where(left, low, swapped(high)), jnp.where(left, swapped(low), high)]
    return pieces


def own_kernel(own_ref, cols_ref, out_ref):
    for zh, piece in enumerate(half_product(own_ref, cols_ref)):
        out_ref[zh] = piece


def join_kernel(core_ref, done_ref, other_ref, cols_ref, out_ref, blocks):
    core = core_ref[0]
    for zh, piece in enumerate(half_product(other_ref, cols_ref)):
        blocks[1 - core, zh] = piece
        blocks[core, zh] = done_ref[zh]
    for z in range(16):
        for xl in range(2):
            for zh in range(4):
                for c in range(2):
                    out_ref[(z * 2 + xl) * 4 + zh, 2 * c : 2 * c + 2, :] = blocks[
                        c, zh, xl * 32 + z * 2 : xl * 32 + z * 2 + 2, :
                    ]


def own_product(own, cols):
    whole = pl.BlockSpec(memory_space=pltpu.VMEM)
    return pl.pallas_call(
        own_kernel,
        in_specs=[whole, whole],
        out_specs=whole,
        out_shape=jax.ShapeDtypeStruct((4, 64, 128), jnp.float32),
        compiler_params=pltpu.CompilerParams(vmem_limit_bytes=24 * 1024 * 1024),
        cost_estimate=pl.CostEstimate(flops=2 * 128 * 256 * SHARE, bytes_accessed=2000000, transcendentals=0),
        name="own_product",
    )(own, cols)


def joined(core, done, other, cols):
    whole = pl.BlockSpec(memory_space=pltpu.VMEM)
    return pl.pallas_call(
        join_kernel,
        in_specs=[pl.BlockSpec(memory_space=pltpu.SMEM), whole, whole, whole],
        out_specs=whole,
        out_shape=jax.ShapeDtypeStruct((128, 4, 128), jnp.float32),
        scratch_shapes=[pltpu.VMEM((2, 4, 64, 128), jnp.float32)],
        compiler_params=pltpu.CompilerParams(vmem_limit_bytes=24 * 1024 * 1024),
        name="joined",
    )(core, done, other, cols)


def finish_kernel(parts_ref, correlation_ref, projected_ref):
    left = lax.broadcasted_iota(jnp.int32, (4, 128), 1) < 64
    pieces = []
    for pair in range(4):
        both = parts_ref[pair]
        for k in range(1, 16):
            both = both + parts_ref[4 * k + pair]
        one, two = both[:4], both[4:]
        low = jnp.where(left, one, swapped(two))
        high = jnp.where(left, swapped(one), two)
        pieces.append(jnp.concatenate([low, high], axis=0))
    given = jnp.concatenate(pieces, axis=1) * (1.0 / (NZ * PLANE))
    at = lax.broadcasted_iota(jnp.int32, (1, 512), 1)

    def field(shift, count):
        return lax.shift_right_logical(at, shift) & (count - 1)

    group = field(3, 2) * 4 + field(1, 4)
    source = group * 64 + field(4, 4) * 16 + field(6, 4) * 4 + field(8, 2) * 2 + field(0, 2)
    hot = jnp.where(lax.broadcasted_iota(jnp.int32, (512, 512), 0) == source, 1.0, 0.0)
    top = given.astype(jnp.bfloat16)
    rest = given - top.astype(jnp.float32)
    middle = rest.astype(jnp.bfloat16)
    last = (rest - middle.astype(jnp.float32)).astype(jnp.bfloat16)
    split = jnp.concatenate(
        [top.astype(jnp.float32), middle.astype(jnp.float32), last.astype(jnp.float32)], axis=0
    )
    placed = jnp.dot(
        split.astype(jnp.bfloat16), hot.astype(jnp.bfloat16), preferred_element_type=jnp.float32
    )
    placed = (placed[16:] + placed[8:16]) + placed[:8]
    correlation_ref[...] = placed[:, :256]
    projected_ref[...] = placed[:, 256:]


def finish(parts):
    shape = jax.ShapeDtypeStruct((8, 256), jnp.float32)
    whole = pl.BlockSpec(memory_space=pltpu.VMEM)
    return pl.pallas_call(
        finish_kernel,
        in_specs=[whole],
        out_specs=[whole, whole],
        out_shape=[shape, shape],
        compiler_params=pltpu.CompilerParams(vmem_limit_bytes=8 * 1024 * 1024),
        name="finish",
    )(parts)


def pieces_kernel(orbitals_ref, potential_ref, out_ref, sems):
    copies = [pltpu.make_async_copy(orbitals_ref, out_ref.at[:, 0:2], sems.at[0])]
    for k in range(4):
        copies.append(pltpu.make_async_copy(potential_ref, out_ref.at[k, 2], sems.at[1 + k]))
    for copy in copies:
        copy.start()
    for copy in copies:
        copy.wait()


def pieces_of(orbitals, potential):
    anywhere = pl.BlockSpec(memory_space=pl.ANY)
    return pl.pallas_call(
        pieces_kernel,
        in_specs=[anywhere, anywhere],
        out_specs=pl.BlockSpec(memory_space=pltpu.VMEM),
        out_shape=jax.ShapeDtypeStruct((4, 3, 2, PLANE), jnp.bfloat16),
        scratch_shapes=[pltpu.SemaphoreType.DMA((5,))],
        compiler_params=pltpu.CompilerParams(vmem_limit_bytes=56 * 1024 * 1024),
        name="pieces",
    )(orbitals, potential)


def per_device(orbitals, boundary, potential):
    own = lax.axis_index("xh") * 2 + lax.axis_index("c")
    pieces = pieces_of(orbitals.reshape(4, 2, 2, PLANE), potential)
    mixed = lax.all_to_all(pieces, ("xh", "c"), split_axis=0, concat_axis=0, tiled=True)
    rim = lax.dynamic_index_in_dim(boundary.reshape(4, 2, 4, PLANE), own, 0, keepdims=False)
    fields = filtered_and_applied(mixed, rim)
    shares = fields.reshape(4, SHARES, SHARE).transpose(1, 0, 2)
    shares = lax.all_to_all(shares, "z", split_axis=0, concat_axis=0, tiled=True)
    cols = shares.reshape(4 * SHARES, SHARE)
    cols = lax.all_to_all(
        jnp.broadcast_to(cols[None], (4, 4 * SHARES, SHARE)), "y", split_axis=0, concat_axis=0, tiled=True
    )
    rows = shares[:, :2].reshape(2 * SHARES, SHARE)
    rows = lax.all_gather(rows, ("xh", "xl"), axis=0, tiled=True)
    other = lax.ppermute(rows, "c", [(0, 1), (1, 0)])
    core = lax.axis_index("c").astype(jnp.int32).reshape(1)
    partial = joined(core, own_product(rows, cols), other, cols)
    parts = lax.all_to_all(partial, ("z", "xl", "xh", "c"), split_axis=0, concat_axis=0, tiled=True)
    return tuple(finish(parts.reshape(64, 8, 128)))


def solution(mesh):
    split = Mesh(mesh.devices.reshape(16, 4, 2, 2, 2), ("z", "y", "xl", "xh", "c"))
    band, domain = ("z", "y", "xl"), ("xh", "c")
    return jax.shard_map(
        per_device,
        mesh=split,
        in_specs=(P(band, domain, None), P(band, None, None), P(domain, None)),
        out_specs=(P(band, domain), P(band, domain)),
        check_vma=False,
    )
```
